128 devices in a mesh: curve: 16 (over z, y), sub: 8 (over x, core).
Axes of the slice: x: 4, y: 4, z: 4, core: 2. Of those that a mesh axis runs over, the one named last changes fastest.
Arguments:
- coarse: float32 [1024, 6, 16, 256], P(('curve', 'sub')), may hold values from -6 to 6
- tags: int32 [1024], P(('curve', 'sub')), may hold values from 0 to 1, as said below
- box_x: int32 [1024], P(('curve', 'sub')), may hold values from 2 to 2049, as said below
- new_counts: int32 [128], P(('curve', 'sub')), may hold values from 1 to 8, as said below
- courant: float32 [6], replicated, may hold values from 0.3 to 0.9
Outputs:
- fine_state: float32 [1024, 6, 32, 1024], P(('curve', 'sub'))
The draws below stay inside these ranges and needn't reach their ends.
Inputs may be any that keep to these rules, and one draw needn't show every extreme that they name: `tags`: each device refines 2 to 8 of its boxes, the first device 1 + 2 or more. `box_x`: along the curve order the refined boxes' values rise strictly; the refined box with id new_start[p] is the right neighbour of the one before it for every device p after the first; boxes that are not refined hold 2049. `new_counts`: they sum to the number of refined boxes; every fine box is owned by the device that holds its coarse box or by a device next to it in curve order; between two such devices at most 2 boxes pass in one direction, and a device keeps at least one of its own; the first device passes exactly 2 boxes to the second.
All inputs are finite; a program needn't handle non-finite values.
Results may differ from the reference program's by a relative error of at most 0.0003.
Values sent between devices are 32-bit elements; how exact they have to be, the bound alone decides.
A program may use at most 64 MiB of HBM per device.

```python
import jax
import jax.numpy as jnp
from jax import lax

CB_DEV = 8
HALF = 16
NF = 6
MOVE = 2
NB = 1024
N_CURVE = 16
N_SUB = 8


def layout(key):
    devices = N_CURVE * N_SUB
    boxes = CB_DEV
    box_total = boxes * devices
    base_key = jax.random.fold_in(key, 411)
    key_count, key_perm = jax.random.split(base_key)
    key_gap = jax.random.fold_in(base_key, 97)
    upper = jnp.where(jnp.arange(devices) == devices - 1, boxes - MOVE, boxes)
    counts = jnp.minimum(jax.random.randint(key_count, (devices,), 2, boxes + 1), upper)
    counts = jnp.where(jnp.arange(devices) == 0, jnp.maximum(counts, MOVE + 1), counts).astype(jnp.int32)
    perm_keys = jax.random.split(key_perm, devices)
    perms = jax.vmap(lambda single: jax.random.permutation(single, boxes))(perm_keys)
    tags = (perms < counts[:, None]).astype(jnp.int32).reshape(-1)
    totals = jnp.sum(counts)
    ends = jnp.cumsum(counts)

    def advance(previous, device):
        own_count = counts[device]
        next_count = counts[device + 1]
        target = (device + 1) * totals // devices - ends[device]
        target = jnp.where(device == 0, -MOVE, target)
        lower = jnp.maximum(jnp.maximum(-MOVE, -own_count), 1 - own_count + previous)
        higher = jnp.minimum(jnp.minimum(MOVE, next_count - 1), boxes - own_count + previous)
        at_last = device == devices - 2
        lower = jnp.where(at_last, jnp.maximum(lower, next_count - boxes), lower)
        chosen_move = jnp.clip(target, lower, higher).astype(jnp.int32)
        return (chosen_move, chosen_move)
    _, boundary_moves = lax.scan(advance, jnp.int32(0), jnp.arange(devices - 1))
    zeros_one = jnp.zeros((1,), jnp.int32)
    new_sizes = (counts + jnp.concatenate([boundary_moves, zeros_one]) - jnp.concatenate([zeros_one, boundary_moves])).astype(jnp.int32)
    new_start = jnp.cumsum(new_sizes) - new_sizes
    boundary = jnp.zeros((box_total,), jnp.int32).at[new_start[1:]].set(1, mode='drop')
    ids = jnp.arange(box_total)
    gap_draw = jax.random.randint(key_gap, (box_total,), 0, 3)
    gaps = jnp.where((gap_draw == 0) & (boundary == 0) & (ids > 0), 1, 0).astype(jnp.int32)
    curve_x = (2 + ids + jnp.cumsum(gaps)).astype(jnp.int32)
    tag_order = jnp.clip(jnp.cumsum(tags) - tags, 0, box_total - 1).astype(jnp.int32)
    box_x = jnp.where(tags == 1, jnp.take(curve_x, tag_order), 2 * box_total + 1).astype(jnp.int32)
    return (tags, new_sizes, box_x)


def draw_tags(key, part):
    return layout(key)[0]


def draw_new_counts(key, part):
    return layout(key)[1]


def draw_box_x(key, part):
    return layout(key)[2]


def block_scale(rng, dims, cuts, least, top_value):
    loudness = 1.0
    for dim, parts in cuts:
        steps = jax.random.uniform(jax.random.fold_in(jax.random.fold_in(rng, 6), dim), (parts,), jnp.float32, least / len(cuts), top_value / len(cuts))
        loudness = loudness * jnp.repeat(jnp.exp(steps), dims[dim] // parts).reshape((-1,) + (1,) * (len(dims) - 1 - dim))
    return loudness


def centred(own_key, dims, deviation, limit, cuts=(), kind=jnp.bfloat16):
    drawn = deviation * jax.random.normal(own_key, dims, jnp.float32)
    if cuts:
        drawn = drawn * block_scale(own_key, dims, cuts, -0.22, 0.18)
    return jnp.clip(drawn, -limit, limit).astype(kind)


def setup_inputs(seed: int = 0) -> dict:
    streams_of = jax.random.split(jax.random.key(seed), 6)
    return {
        "coarse": centred(streams_of[0], (NB, NF, HALF, HALF * HALF), 1.0, 6.0, ((0, 128),), jnp.float32),
        "tags": draw_tags(jax.random.fold_in(streams_of[5], 71), 0),
        "box_x": draw_box_x(jax.random.fold_in(streams_of[5], 71), 0),
        "new_counts": draw_new_counts(jax.random.fold_in(streams_of[5], 71), 0),
        "courant": jnp.clip(jax.random.uniform(streams_of[4], (NF,), jnp.float32, 0.3, 0.9), 0.3, 0.9),
    }


def prolong_table(coarse_len):
    position = jnp.arange(coarse_len)
    identity = (position[:, None] == position[None, :]).astype(jnp.float32)
    ahead = jnp.concatenate([identity[1:], identity[-1:]], 0)
    behind = jnp.concatenate([identity[:1], identity[:-1]], 0)
    at_edge = (position == 0) | (position == coarse_len - 1)
    divisor = jnp.where(at_edge, 1.0, 2.0).astype(jnp.float32)
    slopes = (ahead - behind) / divisor[:, None]
    fine_pos = jnp.arange(2 * coarse_len)
    signs = jnp.where(fine_pos % 2 == 0, -0.25, 0.25).astype(jnp.float32)
    return jnp.repeat(identity, 2, axis=0) + signs[:, None] * jnp.repeat(slopes, 2, axis=0)


def prolong(coarse_boxes):
    box_count = coarse_boxes.shape[0]
    fields = coarse_boxes.shape[1]
    half_len = coarse_boxes.shape[2]
    line_table = prolong_table(half_len)
    plane_table = jnp.kron(line_table, line_table)
    spread = jnp.dot(coarse_boxes.reshape(-1, half_len * half_len), plane_table.T, precision=lax.Precision.HIGHEST)
    spread = spread.reshape(box_count, fields, half_len, 4 * half_len * half_len)
    return jnp.einsum("fx,bcxy->bcfy", line_table, spread, precision=lax.Precision.HIGHEST)


def ppm_step(extended, courant):
    courant_f = courant[None, :, None, None]
    length = extended.shape[2]
    interface = (7.0 / 12.0) * (extended[:, :, 1:length - 2] + extended[:, :, 2:length - 1]) - (1.0 / 12.0) * (extended[:, :, 0:length - 3] + extended[:, :, 3:length])
    left_face = interface[:, :, 0:length - 4]
    right_face = interface[:, :, 1:length - 3]
    centre = extended[:, :, 2:length - 2]
    jump_size = right_face - left_face
    curvature = 6.0 * (centre - 0.5 * (left_face + right_face))
    fluxes = courant_f * (right_face - 0.5 * courant_f * (jump_size - (1.0 - (2.0 / 3.0) * courant_f) * curvature))
    return extended[:, :, 3:length - 2] - (fluxes[:, :, 1:] - fluxes[:, :, :-1])


def ppm_section(state, left_adj, right_adj, courant, devices):
    left_rim = jnp.concatenate([state[:1, :, -3:], state[:-1, :, -3:]], 0)
    left_ghost = jnp.where(left_adj[:, None, None, None], left_rim, state[:, :, :1])
    right_rim = jnp.concatenate([state[1:, :, :2], state[-1:, :, :2]], 0)
    right_ghost = jnp.where(right_adj[:, None, None, None], right_rim, state[:, :, -1:])

    def blocked(array):
        return array.reshape((devices, -1) + array.shape[1:])

    def advance_block(pieces):
        return ppm_step(jnp.concatenate([pieces[0], pieces[1], pieces[2]], 2), courant)

    stepped = lax.map(advance_block, (blocked(left_ghost), blocked(state), blocked(right_ghost)))
    return stepped.reshape(state.shape)


def reference(coarse, tags, box_x, new_counts, courant):
    box_total = coarse.shape[0]
    devices = new_counts.shape[0]
    per_device = box_total // devices
    tag_order = jnp.cumsum(tags) - tags
    live_boxes = jnp.sum(tags)
    target = jnp.where(tags == 1, tag_order, box_total).astype(jnp.int32)
    source = jnp.zeros((box_total,), jnp.int32).at[target].set(jnp.arange(box_total, dtype=jnp.int32), mode="drop")
    packed = coarse[source]
    coords = box_x[source]
    fine_boxes = lax.map(prolong, packed.reshape((devices, per_device) + packed.shape[1:]))
    fine_boxes = fine_boxes.reshape((box_total,) + fine_boxes.shape[2:])
    position = jnp.arange(box_total)
    prev_x = jnp.concatenate([jnp.zeros((1,), jnp.int32), coords[:-1]])
    next_x = jnp.concatenate([coords[1:], jnp.zeros((1,), jnp.int32)])
    left_adj = (position > 0) & (prev_x == coords - 1)
    right_adj = (position + 1 < live_boxes) & (next_x == coords + 1)
    state_one = ppm_section(fine_boxes, left_adj, right_adj, courant, devices)
    state_two = ppm_section(state_one, left_adj, right_adj, courant, devices)
    new_start = jnp.cumsum(new_counts) - new_counts
    slot_ids = jnp.arange(per_device)
    global_ids = (new_start[:, None] + slot_ids[None, :]).reshape(-1)
    occupied = (slot_ids[None, :] < new_counts[:, None]).reshape(-1)
    gathered = state_two[jnp.clip(global_ids, 0, box_total - 1).astype(jnp.int32)]
    return jnp.where(occupied[:, None, None, None], gathered, 0.0)
```

```python
import functools

import jax
import jax.numpy as jnp
import numpy as np
from jax import lax
from jax.experimental import pallas as pl
from jax.experimental.pallas import tpu as pltpu
from jax.sharding import PartitionSpec as P

MESH = pl.DeviceIdType.MESH
LEFT_REACH, RIGHT_REACH = 3, 2


def line_table(coarse_len):
    table = np.zeros((2 * coarse_len, coarse_len), np.float64)
    for cell in range(2 * coarse_len):
        i, sign = cell // 2, (-0.25 if cell % 2 == 0 else 0.25)
        ahead, behind = min(i + 1, coarse_len - 1), max(i - 1, 0)
        table[cell, i] += 1.0
        table[cell, ahead] += sign / (ahead - behind)
        table[cell, behind] -= sign / (ahead - behind)
    return table


def x_tables(half):
    line = line_table(half)
    fine = 2 * half
    wide = np.zeros((3 * fine, 3 * half))
    for box in range(3):
        wide[box * fine : (box + 1) * fine, box * half : (box + 1) * half] = line
    cols = slice(half - 8, 2 * half + 8)
    joined = wide[fine - 2 * LEFT_REACH : 2 * fine + 2 * RIGHT_REACH, cols]
    alone = np.concatenate(
        [wide[fine : fine + 1]] * LEFT_REACH + [wide[fine : 2 * fine]] + [wide[2 * fine - 1 : 2 * fine]] * RIGHT_REACH
    )[:, cols]
    grow = lambda a, rows: np.tile(np.pad(a, ((0, rows - a.shape[0]), (0, 0))), (1, 4)).astype(np.float32)
    return grow(joined, 48), grow(alone, 40)


def step_taps(c):
    c2 = c * c
    c3 = c2 * c
    right, left, own = c - 2.0 * c2 + c3, c3 - c2, 3.0 * c2 - 2.0 * c3
    t = 1.0 / 12.0
    flux = (
        -t * left,
        7.0 * t * left - t * right,
        7.0 * t * (left + right) + own,
        7.0 * t * right - t * left,
        -t * right,
    )
    return (
        flux[0],
        flux[1] - flux[0],
        flux[2] - flux[1],
        1.0 + flux[3] - flux[2],
        flux[4] - flux[3],
        -flux[4],
    )


def split_pair(mat):
    high = mat.astype(jnp.bfloat16)
    low = (mat - high.astype(jnp.float32)).astype(jnp.bfloat16)
    lane = lax.broadcasted_iota(jnp.int32, mat.shape, 1)
    return jnp.where(lane < 64, high.astype(jnp.float32), low.astype(jnp.float32)).astype(jnp.bfloat16)


def exchange(
    n_curve, n_sub,
    tags, box_x, counts, courant, coarse, joined, alone,
    info, from_left, from_right, from_second, mats,
    held, to_right, to_left, to_second, rows, side, first_step,
    load_sem, box_send, box_recv, side_send, side_recv, sub_send, sub_recv, curve_send, curve_recv,
):
    boxes = coarse.shape[0]
    fields = coarse.shape[1]
    fine = 32
    n_half = n_curve // 2
    curve, sub = lax.axis_index("curve"), lax.axis_index("sub")
    me = curve * n_sub + sub
    total = n_curve * n_sub
    upper = curve // n_half
    place = curve % n_half
    after, before = (me + 1) % total, (me + total - 1) % total
    second = (me + 2) % total
    after_id, before_id = (after // n_sub, after % n_sub), (before // n_sub, before % n_sub)
    second_id = (second // n_sub, second % n_sub)
    back = (me + total - 2) % total
    back_id = (back // n_sub, back % n_sub)
    sub_ids = [(curve, (sub + o) % n_sub) for o in range(1, n_sub)]
    curve_ids = [(upper * n_half + (place + o) % n_half, sub) for o in range(1, n_half)]

    barrier = pltpu.get_barrier_semaphore()
    peers = curve_ids + sub_ids + [after_id, before_id, second_id, back_id]
    for peer in peers:
        pl.semaphore_signal(barrier, inc=1, device_id=peer, device_id_type=MESH)
    load = pltpu.make_async_copy(coarse, held, load_sem)
    load.start()

    rank_box = [jnp.int32(0)] * boxes
    seen = jnp.int32(0)
    for b in range(boxes):
        on = tags[b] == 1
        for r in range(b + 1):
            rank_box[r] = jnp.where(on & (seen == r), b, rank_box[r])
        seen = seen + jnp.where(on, 1, 0)
    live = seen

    def box_of(rank):
        found = jnp.int32(0)
        for r in range(boxes):
            found = jnp.where(rank == r, rank_box[r], found)
        return found

    tail_box = [box_of(live - 3 + k) for k in range(3)]
    head_box = [rank_box[k] for k in range(3)]
    lane = lax.broadcasted_iota(jnp.int32, (1, 128), 1)
    row = jnp.where(lane == 0, counts[0] - live, jnp.where(lane == 7, live, 0))
    for k in range(3):
        row = jnp.where(lane == 1 + k, box_x[tail_box[k]], row)
        row = jnp.where(lane == 4 + k, box_x[head_box[k]], row)
    rows[place, sub] = row

    load.wait()
    for f in range(fields):
        at, rim, low = 32 * f, 32 * fields + 8 * (f // 2), 4 * (f % 2)
        to_right[at : at + 16, :] = held[tail_box[1], f]
        to_right[at + 16 : at + 32, :] = held[tail_box[2], f]
        to_right[rim + low : rim + low + 4, :] = held[tail_box[0], f, 12:16, :]
        to_second[rim - 32 * fields + low : rim - 32 * fields + low + 4, :] = held[tail_box[2], f, 12:16, :]
        to_left[at : at + 16, :] = held[head_box[0], f]
        to_left[at + 16 : at + 32, :] = held[head_box[1], f]
        to_left[rim + low : rim + low + 4, :] = held[head_box[2], f, 0:4, :]
    pl.semaphore_wait(barrier, len(peers))

    def send(src, dst, send_sem, recv_sem, peer):
        copy = pltpu.make_async_remote_copy(
            src_ref=src, dst_ref=dst, send_sem=send_sem, recv_sem=recv_sem, device_id=peer, device_id_type=MESH
        )
        copy.start()
        return copy

    mine = rows.at[place, sub]
    sub_copies = [send(mine, mine, sub_send.at[o], sub_recv.at[o], peer) for o, peer in enumerate(sub_ids)]
    side_copies = [
        send(mine, side.at[0], side_send.at[0], side_recv.at[0], after_id),
        send(mine, side.at[1], side_send.at[1], side_recv.at[1], before_id),
        send(mine, side.at[2], side_send.at[2], side_recv.at[2], second_id),
    ]
    box_copies = [
        send(to_right, from_left, box_send.at[0], box_recv.at[0], after_id),
        send(to_left, from_right, box_send.at[1], box_recv.at[1], before_id),
        send(to_second, from_second, box_send.at[2], box_recv.at[2], second_id),
    ]

    for copy in sub_copies:
        copy.wait_recv()
    group = rows.at[place]
    curve_copies = [
        send(group, group, curve_send.at[o], curve_recv.at[o], peer) for o, peer in enumerate(curve_ids)
    ]

    for f in range(fields):
        taps = step_taps(courant[f])
        both = []
        for s in range(11):
            terms = [taps[m] * taps[s - m] for m in range(6) if 0 <= s - m < 6]
            both.append(functools.reduce(lambda a, b: a + b, terms))
        mat = both[0] * joined[0:fine, :]
        for s in range(1, 11):
            mat = mat + both[s] * joined[s : s + fine, :]
        mats[f, 1] = split_pair(mat)
        one = taps[0] * alone[0:fine, :]
        for s in range(1, 6):
            one = one + taps[s] * alone[s : s + fine, :]
        first_step[0:8, :] = jnp.broadcast_to(one[0:1, :], (8, 128))
        first_step[8 : 8 + fine, :] = one
        first_step[8 + fine : 16 + fine, :] = jnp.broadcast_to(one[fine - 1 : fine, :], (8, 128))
        two = taps[0] * first_step[5 : 5 + fine, :]
        for s in range(1, 6):
            two = two + taps[s] * first_step[5 + s : 5 + s + fine, :]
        mats[f, 0] = split_pair(two)
        mats[f, 2] = jnp.zeros((fine, 128), jnp.bfloat16)

    for copy in side_copies:
        copy.wait_recv()
    left_row, right_row, second_row = side[0], side[1], side[2]
    left_x = [jnp.sum(jnp.where(lane == 1 + k, left_row, 0)) for k in range(3)]
    short = jnp.sum(jnp.where(lane == 7, left_row, 0)) < 3
    left_x[0] = jnp.where(short, jnp.sum(jnp.where(lane == 3, second_row, 0)), left_x[0])
    info[12] = jnp.where(short, 1, 0)
    right_x = [jnp.sum(jnp.where(lane == 4 + k, right_row, 0)) for k in range(3)]

    for copy in curve_copies:
        copy.wait_recv()
    shape = rows.shape
    order = lax.broadcasted_iota(jnp.int32, shape, 0) * n_sub + lax.broadcasted_iota(jnp.int32, shape, 1)
    lanes = lax.broadcasted_iota(jnp.int32, shape, 3)
    spot = place * n_sub + sub
    below = jnp.where((lanes == 0) & (order < spot), rows[...], 0)
    above = jnp.where((lanes == 0) & (order >= spot), rows[...], 0)
    offset = jnp.sum(jnp.where(upper == 0, below, -above))

    def coord_of(rank):
        found = left_x[0]
        for k in range(3):
            found = jnp.where(rank == k - 3, left_x[k], found)
        for r in range(boxes):
            found = jnp.where((rank == r) & (rank < live), box_x[rank_box[r]], found)
        for k in range(3):
            found = jnp.where(rank == live + k, right_x[k], found)
        return found

    def start_of(rank):
        inside = 40 + 16 * box_of(rank)
        return jnp.where(rank < 0, 40 + 16 * rank, jnp.where(rank < live, inside, 168 + 16 * (rank - live)))

    ranks = [jnp.clip(offset + j, -3, live + 2) for j in range(-1, boxes + 1)]
    coords = [coord_of(r) for r in ranks]
    for j in range(boxes + 2):
        info[j] = start_of(ranks[j])
    for j in range(boxes):
        rank = ranks[j + 1]
        used = j < counts[0]
        on_left = (coords[j] == coords[j + 1] - 1) & ((me > 0) | (rank > 0))
        on_right = (coords[j + 2] == coords[j + 1] + 1) & ((me < total - 1) | (rank < live - 1))
        info[16 + j] = jnp.where(used, jnp.where(on_left, 1, 0), 2)
        info[24 + j] = jnp.where(used, jnp.where(on_right, 1, 0), 2)

    for copy in box_copies:
        copy.wait_recv()
    for copy in sub_copies + side_copies + box_copies + curve_copies:
        copy.wait_send()


def refine(info, coarse, left_boxes, left_rim, second_rim, right_boxes, right_rim, mats, table, out, line):
    boxes = coarse.shape[0]
    even = pl.program_id(0) % 2 == 0
    rim = jnp.where(info[12] == 1, second_rim[...], left_rim[...])
    line[0:8, :] = jnp.where(even, pltpu.roll(rim, 4, 0), rim)
    line[8:40, :] = left_boxes[...]
    for b in range(boxes):
        line[40 + 16 * b : 56 + 16 * b, :] = coarse[b, 0]
    line[168:200, :] = right_boxes[...]
    rim = right_rim[...]
    rim = jnp.where(even, rim, pltpu.roll(rim, 4, 0))
    line[200:208, :] = rim
    line[208:216, :] = rim
    parts = []
    for j in range(boxes):
        at = pl.multiple_of(info[j + 1], 8)
        left_at = pl.multiple_of(info[j] + 8, 8)
        right_at = pl.multiple_of(info[j + 2], 8)
        data = jnp.concatenate(
            [line[pl.ds(left_at, 8), :], line[pl.ds(at, 16), :], line[pl.ds(right_at, 8), :]], axis=0
        )
        high = data.astype(jnp.bfloat16)
        low = (data - high.astype(jnp.float32)).astype(jnp.bfloat16)
        stacked = jnp.concatenate([high, low, high, low], axis=0)
        mat = jnp.concatenate([mats[0, info[16 + j], 0:16, :], mats[0, info[24 + j], 16:32, :]], axis=0)
        parts.append(jnp.dot(mat, stacked, preferred_element_type=jnp.float32))
    moved = jnp.concatenate(parts, axis=0)
    high = moved.astype(jnp.bfloat16)
    low = (moved - high.astype(jnp.float32)).astype(jnp.bfloat16)
    spread = jnp.dot(high, table[...], preferred_element_type=jnp.float32)
    spread = spread + jnp.dot(low, table[...], preferred_element_type=jnp.float32)
    out[...] = spread.reshape(out.shape)


def local(n_curve, n_sub, coarse, tags, box_x, counts, courant):
    boxes, fields, half, plane = coarse.shape
    fine = 2 * half
    joined, alone = x_tables(half)
    line = line_table(half)
    table = jnp.asarray(np.kron(line, line).T, jnp.bfloat16)
    smem = pl.BlockSpec(memory_space=pltpu.SMEM)
    vmem = pl.BlockSpec(memory_space=pltpu.VMEM)
    anywhere = pl.BlockSpec(memory_space=pl.ANY)
    packed = 32 * fields + 4 * fields
    edge = jax.ShapeDtypeStruct((packed, plane), jnp.float32)
    dma = pltpu.SemaphoreType.DMA
    n_half = n_curve // 2
    info, from_left, from_right, from_second, mats = pl.pallas_call(
        functools.partial(exchange, n_curve, n_sub),
        out_shape=(
            jax.ShapeDtypeStruct((32,), jnp.int32),
            edge,
            edge,
            jax.ShapeDtypeStruct((4 * fields, plane), jnp.float32),
            jax.ShapeDtypeStruct((fields, 3, fine, 128), jnp.bfloat16),
        ),
        in_specs=[smem, smem, smem, smem, anywhere, vmem, vmem],
        out_specs=(smem, anywhere, anywhere, anywhere, vmem),
        scratch_shapes=[
            pltpu.VMEM(coarse.shape, jnp.float32),
            pltpu.VMEM((packed, plane), jnp.float32),
            pltpu.VMEM((packed, plane), jnp.float32),
            pltpu.VMEM((4 * fields, plane), jnp.float32),
            pltpu.VMEM((n_half, n_sub, 1, 128), jnp.int32),
            pltpu.VMEM((3, 1, 128), jnp.int32),
            pltpu.VMEM((48, 128), jnp.float32),
            dma,
            dma((3,)),
            dma((3,)),
            dma((3,)),
            dma((3,)),
            dma((n_sub - 1,)),
            dma((n_sub - 1,)),
            dma((n_half - 1,)),
            dma((n_half - 1,)),
        ],
        compiler_params=pltpu.CompilerParams(collective_id=0, has_side_effects=True),
        name="exchange",
    )(tags, box_x, counts, courant, coarse, jnp.asarray(joined), jnp.asarray(alone))
    return pl.pallas_call(
        refine,
        out_shape=jax.ShapeDtypeStruct((boxes, fields, fine, 4 * plane), jnp.float32),
        grid=(fields,),
        in_specs=[
            smem,
            pl.BlockSpec((boxes, 1, half, plane), lambda f: (0, f, 0, 0)),
            pl.BlockSpec((32, plane), lambda f: (f, 0)),
            pl.BlockSpec((8, plane), lambda f: (4 * fields + f // 2, 0)),
            pl.BlockSpec((8, plane), lambda f: (f // 2, 0)),
            pl.BlockSpec((32, plane), lambda f: (f, 0)),
            pl.BlockSpec((8, plane), lambda f: (4 * fields + f // 2, 0)),
            pl.BlockSpec((1, 3, fine, 128), lambda f: (f, 0, 0, 0)),
            pl.BlockSpec((plane, 4 * plane), lambda f: (0, 0)),
        ],
        out_specs=pl.BlockSpec((boxes, 1, fine, 4 * plane), lambda f: (0, f, 0, 0)),
        scratch_shapes=[pltpu.VMEM((216, plane), jnp.float32)],
        name="refine",
    )(info, coarse, from_left, from_left, from_second, from_right, from_right, mats, table)


def solution(mesh):
    both = ("curve", "sub")
    in_specs = (P(both, None, None, None), P(both), P(both), P(both), P())
    return jax.shard_map(
        functools.partial(local, mesh.shape["curve"], mesh.shape["sub"]),
        mesh=mesh,
        in_specs=in_specs,
        out_specs=P(both, None, None, None),
        check_vma=False,
    )
```

```python
import functools

import jax
import jax.numpy as jnp
import numpy as np
from jax import lax
from jax.experimental import pallas as pl
from jax.experimental.pallas import tpu as pltpu
from jax.sharding import PartitionSpec as P

MESH = pl.DeviceIdType.MESH
MOVE = 2
LEFT_REACH, RIGHT_REACH = 3, 2


def line_table(coarse_len):
    table = np.zeros((2 * coarse_len, coarse_len), np.float64)
    for cell in range(2 * coarse_len):
        i, sign = cell // 2, (-0.25 if cell % 2 == 0 else 0.25)
        ahead, behind = min(i + 1, coarse_len - 1), max(i - 1, 0)
        table[cell, i] += 1.0
        table[cell, ahead] += sign / (ahead - behind)
        table[cell, behind] -= sign / (ahead - behind)
    return table


def x_tables(half):
    line = line_table(half)
    fine = 2 * half
    wide = np.zeros((3 * fine, 3 * half))
    for box in range(3):
        wide[box * fine : (box + 1) * fine, box * half : (box + 1) * half] = line
    cols = np.concatenate([2 * half + np.arange(4), half - 4 + np.arange(4), half + np.arange(half)])
    joined = wide[fine - 2 * LEFT_REACH : 2 * fine + 2 * RIGHT_REACH, cols]
    alone = np.concatenate(
        [wide[fine : fine + 1]] * LEFT_REACH + [wide[fine : 2 * fine]] + [wide[2 * fine - 1 : 2 * fine]] * RIGHT_REACH
    )[:, cols]

    def grow(a, rows):
        a = np.tile(np.pad(a, ((0, rows - a.shape[0]), (0, 0))), (1, 4))
        return np.pad(a, ((0, 0), (0, 128 - a.shape[1]))).astype(np.float32)

    return grow(joined, 48), grow(alone, 40)


def plane_tables(half):
    line = line_table(half)
    table = np.kron(line, line).T
    size = half * half
    lane = np.arange(size // 2)
    picks = [lane, np.where(lane < 32, lane + 128, lane), np.where(lane < 96, lane + 128, lane), lane + 128]
    quarters = []
    for n, pick in enumerate(picks):
        columns = table[:, n * size : (n + 1) * size]
        missed = np.delete(columns, pick, axis=0)
        assert not missed.any()
        quarters.append(np.concatenate([columns[pick], columns[pick]]))
    return np.stack(quarters)


def step_taps(c):
    c2 = c * c
    c3 = c2 * c
    right, left, own = c - 2.0 * c2 + c3, c3 - c2, 3.0 * c2 - 2.0 * c3
    t = 1.0 / 12.0
    flux = (
        -t * left,
        7.0 * t * left - t * right,
        7.0 * t * (left + right) + own,
        7.0 * t * right - t * left,
        -t * right,
    )
    return (
        flux[0],
        flux[1] - flux[0],
        flux[2] - flux[1],
        1.0 + flux[3] - flux[2],
        flux[4] - flux[3],
        -flux[4],
    )


def split_pair(mat):
    high = mat.astype(jnp.bfloat16).astype(jnp.float32)
    lane = lax.broadcasted_iota(jnp.int32, mat.shape, 1)
    return jnp.where(lane < 48, high, mat - high).astype(jnp.bfloat16)


def exchange(
    n_curve, n_sub,
    tags_in, box_x_in, counts_in, courant_in, coarse, joined_in, alone_in,
    info_out, all_rows, from_left, from_right, from_second, mats_out,
    tags, box_x, counts, courant, info, joined, alone, mats,
    held, to_right, to_left, to_second, rows, side, first_step,
    load_sem, out_sem, box_send, box_recv, side_send, side_recv, sub_send, sub_recv, curve_send, curve_recv,
):
    boxes = coarse.shape[0]
    fields = coarse.shape[1]
    fine = 32
    n_half = n_curve // 2
    curve, sub = lax.axis_index("curve"), lax.axis_index("sub")
    me = curve * n_sub + sub
    total = n_curve * n_sub
    upper = curve // n_half
    place = curve % n_half

    def device(index):
        return (index // n_sub, index % n_sub)

    sub_ids = [(curve, (sub + o) % n_sub) for o in range(1, n_sub)]
    curve_ids = [(upper * n_half + (place + o) % n_half, sub) for o in range(1, n_half)]
    chain = [(1, me < total - 1, me > 0), (-1, me > 0, me < total - 1), (2, me < total - 2, me > 1)]

    barrier = pltpu.get_barrier_semaphore()

    def signal(peer):
        pl.semaphore_signal(barrier, inc=1, device_id=peer, device_id_type=MESH)

    loads = [
        pltpu.make_async_copy(a, b, load_sem.at[k])
        for k, (a, b) in enumerate(
            [
                (coarse, held), (tags_in, tags), (box_x_in, box_x), (counts_in, counts), (courant_in, courant),
                (joined_in, joined), (alone_in, alone),
            ]
        )
    ]
    for load in loads:
        load.start()
    for peer in curve_ids + sub_ids:
        signal(peer)
    expected = jnp.int32(len(curve_ids) + len(sub_ids))
    for step, sends, gets in chain + [(-2, me > 1, me < total - 2)]:
        @pl.when(sends)
        def _(step=step):
            signal(device(me + step))
        expected = expected + jnp.where(gets, 1, 0)

    for load in loads[1:4]:
        load.wait()
    rank_box = [jnp.int32(0)] * boxes
    seen = jnp.int32(0)
    for b in range(boxes):
        on = tags[b] == 1
        for r in range(b + 1):
            rank_box[r] = jnp.where(on & (seen == r), b, rank_box[r])
        seen = seen + jnp.where(on, 1, 0)
    live = seen

    def box_of(rank):
        found = jnp.int32(0)
        for r in range(boxes):
            found = jnp.where(rank == r, rank_box[r], found)
        return found

    tail_box = [box_of(live - 3 + k) for k in range(3)]
    head_box = [rank_box[k] for k in range(3)]
    lane = lax.broadcasted_iota(jnp.int32, (1, 128), 1)
    row = jnp.where(lane == 0, counts[0] - live, jnp.where(lane == 7, live, 0))
    for k in range(3):
        row = jnp.where(lane == 1 + k, box_x[tail_box[k]], row)
        row = jnp.where(lane == 4 + k, box_x[head_box[k]], row)
    rows[place, sub] = row

    loads[0].wait()
    for f in range(fields):
        at, rim, low = 32 * f, 32 * fields + 8 * (f // 2), 4 * (f % 2)
        to_right[at : at + 16, :] = held[tail_box[1], f]
        to_right[at + 16 : at + 32, :] = held[tail_box[2], f]
        to_right[rim + low : rim + low + 4, :] = held[tail_box[0], f, 12:16, :]
        to_second[rim - 32 * fields + low : rim - 32 * fields + low + 4, :] = held[tail_box[2], f, 12:16, :]
        to_left[at : at + 16, :] = held[head_box[0], f]
        to_left[at + 16 : at + 32, :] = held[head_box[1], f]
        to_left[rim + low : rim + low + 4, :] = held[head_box[2], f, 0:4, :]
    pl.semaphore_wait(barrier, expected)

    def copy_to(src, dst, send_sem, recv_sem, peer):
        return pltpu.make_async_remote_copy(
            src_ref=src, dst_ref=dst, send_sem=send_sem, recv_sem=recv_sem, device_id=peer, device_id_type=MESH
        )

    mine, group = rows.at[place, sub], rows.at[place]
    sub_copies = [copy_to(mine, mine, sub_send.at[o], sub_recv.at[o], peer) for o, peer in enumerate(sub_ids)]
    curve_copies = [
        copy_to(group, all_rows.at[place], curve_send.at[o], curve_recv.at[o], peer)
        for o, peer in enumerate(curve_ids)
    ]
    box_ends = [(to_right, from_left), (to_left, from_right), (to_second, from_second)]
    box_copies = []
    side_copies = []
    for k, (step, sends, gets) in enumerate(chain):
        peer = device(jnp.clip(me + step, 0, total - 1))
        box_copies.append(copy_to(*box_ends[k], box_send.at[k], box_recv.at[k], peer))
        side_copies.append(copy_to(mine, side.at[k], side_send.at[k], side_recv.at[k], peer))
    for copy in sub_copies:
        copy.start()
    for k, (step, sends, gets) in enumerate(chain):
        @pl.when(sends)
        def _(k=k):
            side_copies[k].start()
            box_copies[k].start()

    for copy in sub_copies:
        copy.wait_recv()
    for copy in curve_copies:
        copy.start()
    keep = pltpu.make_async_copy(group, all_rows.at[place], out_sem.at[0])
    keep.start()

    for load in loads[4:]:
        load.wait()
    for f in range(fields):
        taps = step_taps(courant[f])
        both = []
        for s in range(11):
            terms = [taps[m] * taps[s - m] for m in range(6) if 0 <= s - m < 6]
            both.append(functools.reduce(lambda a, b: a + b, terms))
        mat = both[0] * joined[0:fine, :]
        for s in range(1, 11):
            mat = mat + both[s] * joined[s : s + fine, :]
        mats[f, 1] = split_pair(mat)
        one = taps[0] * alone[0:fine, :]
        for s in range(1, 6):
            one = one + taps[s] * alone[s : s + fine, :]
        first_step[0:8, :] = jnp.broadcast_to(one[0:1, :], (8, 128))
        first_step[8 : 8 + fine, :] = one
        first_step[8 + fine : 16 + fine, :] = jnp.broadcast_to(one[fine - 1 : fine, :], (8, 128))
        two = taps[0] * first_step[5 : 5 + fine, :]
        for s in range(1, 6):
            two = two + taps[s] * first_step[5 + s : 5 + s + fine, :]
        mats[f, 0] = split_pair(two)
        mats[f, 2] = jnp.zeros((fine, 128), jnp.bfloat16)
    save_mats = pltpu.make_async_copy(mats, mats_out, out_sem.at[1])
    save_mats.start()

    for k, (step, sends, gets) in enumerate(chain):
        @pl.when(gets)
        def _(k=k):
            side_copies[k].wait_recv()
    right_row, left_row, second_row = side[1], side[0], side[2]
    left_x = [jnp.sum(jnp.where(lane == 1 + k, left_row, 0)) for k in range(3)]
    short = jnp.sum(jnp.where(lane == 7, left_row, 0)) < 3
    left_x[0] = jnp.where(short, jnp.sum(jnp.where(lane == 3, second_row, 0)), left_x[0])
    right_x = [jnp.sum(jnp.where(lane == 4 + k, right_row, 0)) for k in range(3)]
    last = total - 1
    coord_before = jnp.int32(0)
    for k in range(boxes + 2 * MOVE + 2):
        rank = k - 3
        if rank < 0:
            start = jnp.int32(40 + 16 * rank)
            coord = jnp.where(me > 0, left_x[k], -8)
        else:
            past = rank - live
            own_box = rank_box[rank] if rank < boxes else jnp.int32(0)
            start = jnp.where(past < 0, 40 + 16 * own_box, 168 + 16 * jnp.minimum(past, 2))
            beyond = jnp.where(past == 0, right_x[0], jnp.where(past == 1, right_x[1], right_x[2]))
            beyond = jnp.where(me < last, beyond, -8)
            coord = jnp.where(past < 0, box_x[own_box], beyond)
        info[k] = start
        info[16 + k] = jnp.where(coord_before + 1 == coord, 1, 0) if k else 0
        coord_before = coord
    info[14] = jnp.where(short, 1, 0)
    info[15] = counts[0]
    save_info = pltpu.make_async_copy(info, info_out, out_sem.at[2])
    save_info.start()

    save_mats.wait()
    save_info.wait()
    keep.wait()
    for copy in curve_copies:
        copy.wait_recv()
    for k, (step, sends, gets) in enumerate(chain):
        @pl.when(gets)
        def _(k=k):
            box_copies[k].wait_recv()
    for copy in sub_copies + curve_copies:
        copy.wait_send()
    for k, (step, sends, gets) in enumerate(chain):
        @pl.when(sends)
        def _(k=k):
            side_copies[k].wait_send()
            box_copies[k].wait_send()


def refine(
    n_curve, n_sub,
    info, all_rows, coarse, from_left, from_right, from_second, mats_in, tables_in,
    out,
    line, mats, tables, windows, stage, load_sem, out_sem,
):
    boxes, fields = coarse.shape[:2]
    n_half = n_curve // 2
    loads = []

    def load(src, dst):
        copy = pltpu.make_async_copy(src, dst, load_sem.at[len(loads)])
        copy.start()
        loads.append(copy)

    for b in range(boxes):
        load(coarse.at[b], line.at[:, 40 + 16 * b : 56 + 16 * b, :])
    load(mats_in, mats)
    for f in range(fields):
        load(from_left.at[32 * f : 32 * f + 32], line.at[f, 8:40])
        load(from_right.at[32 * f : 32 * f + 32], line.at[f, 168:200])
    edges = slice(32 * fields, 36 * fields)
    load(from_left.at[edges], stage.at[0, 0, 0 : 4 * fields, 0:256])
    load(from_second, stage.at[0, 1, 0 : 4 * fields, 0:256])
    load(from_right.at[edges], stage.at[0, 2, 0 : 4 * fields, 0:256])
    load(tables_in, tables)

    curve, sub = lax.axis_index("curve"), lax.axis_index("sub")
    shape = all_rows.shape
    order = lax.broadcasted_iota(jnp.int32, shape, 0)
    lanes = lax.broadcasted_iota(jnp.int32, shape, 1)
    spot = (curve % n_half) * n_sub + sub
    below = jnp.where((lanes == 0) & (order < spot), all_rows[...], 0)
    above = jnp.where((lanes == 0) & (order >= spot), all_rows[...], 0)
    offset = jnp.sum(jnp.where(curve < n_half, below, -above))
    wanted = info[15]
    starts, left_starts, right_starts, left_on, right_on, left_mat, right_mat = [], [], [], [], [], [], []
    for j in range(boxes):
        at = offset + 3 + j
        used = j < wanted
        starts.append(pl.multiple_of(jnp.where(used, info[at], 40), 8))
        left_starts.append(pl.multiple_of(info[at - 1] + 8, 8))
        right_starts.append(pl.multiple_of(info[at + 1], 8))
        left_on.append(info[16 + at])
        right_on.append(info[17 + at])
        left_mat.append(jnp.where(used, left_on[j], 2))
        right_mat.append(jnp.where(used, right_on[j], 2))

    for copy in loads:
        copy.wait()
    for pair in range(fields // 2):
        cut = slice(8 * pair, 8 * pair + 8)
        left_rim = jnp.where(info[14] == 1, stage[0, 1, cut, 0:256], stage[0, 0, cut, 0:256])
        right_rim = stage[0, 2, cut, 0:256]
        line[2 * pair, 0:8, :] = pltpu.roll(left_rim, 4, 0)
        line[2 * pair + 1, 0:8, :] = left_rim
        line[2 * pair, 200:208, :] = right_rim
        line[2 * pair + 1, 200:208, :] = pltpu.roll(right_rim, 4, 0)

    top = lax.broadcasted_iota(jnp.int32, (8, 256), 0) < 4
    lane = lax.broadcasted_iota(jnp.int32, (32, 128), 1)

    def along_x(f):
        for j in range(boxes):
            left = jnp.where(left_on[j] == 1, line[f, pl.ds(left_starts[j], 8), :], 0.0)
            right = jnp.where(right_on[j] == 1, line[f, pl.ds(right_starts[j], 8), :], 0.0)
            data = jnp.concatenate([jnp.where(top, right, left), line[f, pl.ds(starts[j], 16), :]], axis=0)
            rest = data - data.astype(jnp.bfloat16).astype(jnp.float32)
            stacked = jnp.concatenate([data, rest], axis=0).astype(jnp.bfloat16)
            stacked = jnp.concatenate([stacked, stacked], axis=0)
            mat = jnp.concatenate([mats[f, left_mat[j], 0:16, :], mats[f, right_mat[j], 16:32, :]], axis=0)
            moved = jnp.dot(mat[:, 0:96], stacked, preferred_element_type=jnp.float32)
            a, b = moved[:, 0:128], moved[:, 128:256]
            for n, part in enumerate([a, jnp.where(lane < 32, b, a), jnp.where(lane < 96, b, a), b]):
                high = part.astype(jnp.bfloat16)
                windows[f % 2, n, 32 * j : 32 * j + 32, 0:128] = high
                windows[f % 2, n, 32 * j : 32 * j + 32, 128:256] = (part - high.astype(jnp.float32)).astype(jnp.bfloat16)

    copies = []
    along_x(0)
    for f in range(fields):
        if f + 1 < fields:
            along_x(f + 1)
        for n in range(4):
            spread = jnp.dot(windows[f % 2, n], tables[n], preferred_element_type=jnp.float32)
            stage[f, :, :, 256 * n : 256 * n + 256] = spread.reshape(boxes, 32, 256)
        copy = pltpu.make_async_copy(stage.at[f], out.at[:, f], out_sem.at[f])
        copy.start()
        copies.append(copy)
    for copy in copies:
        copy.wait()


def local(n_curve, n_sub, coarse, tags, box_x, counts, courant):
    boxes, fields, half, plane = coarse.shape
    fine = 2 * half
    joined, alone = x_tables(half)
    tables = jnp.asarray(plane_tables(half), jnp.bfloat16)
    smem = pl.BlockSpec(memory_space=pltpu.SMEM)
    vmem = pl.BlockSpec(memory_space=pltpu.VMEM)
    anywhere = pl.BlockSpec(memory_space=pl.ANY)
    packed = 36 * fields
    edge = jax.ShapeDtypeStruct((packed, plane), jnp.float32)
    dma = pltpu.SemaphoreType.DMA
    n_half = n_curve // 2
    mats_shape = (fields, 3, fine, 128)
    info, all_rows, from_left, from_right, from_second, mats = pl.pallas_call(
        functools.partial(exchange, n_curve, n_sub),
        out_shape=(
            jax.ShapeDtypeStruct((32,), jnp.int32),
            jax.ShapeDtypeStruct((n_half, n_sub, 1, 128), jnp.int32),
            edge,
            edge,
            jax.ShapeDtypeStruct((4 * fields, plane), jnp.float32),
            jax.ShapeDtypeStruct(mats_shape, jnp.bfloat16),
        ),
        in_specs=[anywhere] * 7,
        out_specs=(anywhere,) * 6,
        scratch_shapes=[
            pltpu.SMEM((boxes,), jnp.int32),
            pltpu.SMEM((boxes,), jnp.int32),
            pltpu.SMEM((1,), jnp.int32),
            pltpu.SMEM((fields,), jnp.float32),
            pltpu.SMEM((32,), jnp.int32),
            pltpu.VMEM((48, 128), jnp.float32),
            pltpu.VMEM((40, 128), jnp.float32),
            pltpu.VMEM(mats_shape, jnp.bfloat16),
            pltpu.VMEM(coarse.shape, jnp.float32),
            pltpu.VMEM((packed, plane), jnp.float32),
            pltpu.VMEM((packed, plane), jnp.float32),
            pltpu.VMEM((4 * fields, plane), jnp.float32),
            pltpu.VMEM((n_half, n_sub, 1, 128), jnp.int32),
            pltpu.VMEM((3, 1, 128), jnp.int32),
            pltpu.VMEM((48, 128), jnp.float32),
            dma((7,)),
            dma((3,)),
            dma((3,)),
            dma((3,)),
            dma((3,)),
            dma((3,)),
            dma((n_sub - 1,)),
            dma((n_sub - 1,)),
            dma((n_half - 1,)),
            dma((n_half - 1,)),
        ],
        compiler_params=pltpu.CompilerParams(collective_id=0, has_side_effects=True),
        name="exchange",
    )(tags, box_x, counts, courant, coarse, jnp.asarray(joined), jnp.asarray(alone))
    return pl.pallas_call(
        functools.partial(refine, n_curve, n_sub),
        out_shape=jax.ShapeDtypeStruct((boxes, fields, fine, 4 * plane), jnp.float32),
        in_specs=[smem, vmem] + [anywhere] * 6,
        out_specs=anywhere,
        scratch_shapes=[
            pltpu.VMEM((fields, 216, plane), jnp.float32),
            pltpu.VMEM(mats_shape, jnp.bfloat16),
            pltpu.VMEM(tables.shape, jnp.bfloat16),
            pltpu.VMEM((2, 4, boxes * fine, plane), jnp.bfloat16),
            pltpu.VMEM((fields, boxes, fine, 4 * plane), jnp.float32),
            dma((boxes + 5 + 2 * fields,)),
            dma((fields,)),
        ],
        name="refine",
    )(info, all_rows.reshape(n_half * n_sub, 128), coarse, from_left, from_right, from_second, mats, tables)


def solution(mesh):
    both = ("curve", "sub")
    in_specs = (P(both, None, None, None), P(both), P(both), P(both), P())
    return jax.shard_map(
        functools.partial(local, mesh.shape["curve"], mesh.shape["sub"]),
        mesh=mesh,
        in_specs=in_specs,
        out_specs=P(both, None, None, None),
        check_vma=False,
    )
```

```python
import functools

import jax
import jax.numpy as jnp
import numpy as np
from jax import lax
from jax.experimental import pallas as pl
from jax.experimental.pallas import tpu as pltpu
from jax.sharding import PartitionSpec as P

MESH = pl.DeviceIdType.MESH
MOVE = 2
LEFT_REACH, RIGHT_REACH = 3, 2


def line_table(coarse_len):
    table = np.zeros((2 * coarse_len, coarse_len), np.float64)
    for cell in range(2 * coarse_len):
        i, sign = cell // 2, (-0.25 if cell % 2 == 0 else 0.25)
        ahead, behind = min(i + 1, coarse_len - 1), max(i - 1, 0)
        table[cell, i] += 1.0
        table[cell, ahead] += sign / (ahead - behind)
        table[cell, behind] -= sign / (ahead - behind)
    return table


def x_tables(half):
    line = line_table(half)
    fine = 2 * half
    wide = np.zeros((3 * fine, 3 * half))
    for box in range(3):
        wide[box * fine : (box + 1) * fine, box * half : (box + 1) * half] = line
    cols = np.concatenate([2 * half + np.arange(4), half - 4 + np.arange(4), half + np.arange(half)])
    joined = wide[fine - 2 * LEFT_REACH : 2 * fine + 2 * RIGHT_REACH, cols]
    alone = np.concatenate(
        [wide[fine : fine + 1]] * LEFT_REACH + [wide[fine : 2 * fine]] + [wide[2 * fine - 1 : 2 * fine]] * RIGHT_REACH
    )[:, cols]

    def grow(a, rows):
        a = np.tile(np.pad(a, ((0, rows - a.shape[0]), (0, 0))), (1, 4))
        return np.pad(a, ((0, 0), (0, 128 - a.shape[1]))).astype(np.float32)

    return grow(joined, 48), grow(alone, 40)


def plane_tables(half):
    line = line_table(half)
    table = np.kron(line, line).T
    size = half * half
    lane = np.arange(size // 2)
    picks = [lane, np.where(lane < 32, lane + 128, lane), np.where(lane < 96, lane + 128, lane), lane + 128]
    quarters = []
    for n, pick in enumerate(picks):
        columns = table[:, n * size : (n + 1) * size]
        missed = np.delete(columns, pick, axis=0)
        assert not missed.any()
        quarters.append(np.concatenate([columns[pick], columns[pick]]))
    return np.stack(quarters)


def step_taps(c):
    c2 = c * c
    c3 = c2 * c
    right, left, own = c - 2.0 * c2 + c3, c3 - c2, 3.0 * c2 - 2.0 * c3
    t = 1.0 / 12.0
    flux = (
        -t * left,
        7.0 * t * left - t * right,
        7.0 * t * (left + right) + own,
        7.0 * t * right - t * left,
        -t * right,
    )
    return (
        flux[0],
        flux[1] - flux[0],
        flux[2] - flux[1],
        1.0 + flux[3] - flux[2],
        flux[4] - flux[3],
        -flux[4],
    )


def split_pair(mat):
    high = mat.astype(jnp.bfloat16).astype(jnp.float32)
    lane = lax.broadcasted_iota(jnp.int32, mat.shape, 1)
    return jnp.where(lane < 48, high, mat - high).astype(jnp.bfloat16)


def exchange(
    n_curve, n_sub,
    tags_in, box_x_in, courant_in, coarse, joined_in, alone_in, tables_in, counts,
    all_rows, cand,
    tags, box_x, courant, joined, alone, tables, mats, windows,
    held, to_right, to_left, to_second, from_left, from_right, from_second, rows, side, first_step,
    load_sem, out_sem, box_send, box_recv, side_send, side_recv, sub_send, sub_recv, curve_send, curve_recv,
):
    boxes = coarse.shape[0]
    fields = coarse.shape[1]
    fine = 32
    n_half = n_curve // 2
    curve, sub = lax.axis_index("curve"), lax.axis_index("sub")
    me = curve * n_sub + sub
    total = n_curve * n_sub
    upper = curve // n_half
    place = curve % n_half

    def device(index):
        return (index // n_sub, index % n_sub)

    sub_ids = [(curve, (sub + o) % n_sub) for o in range(1, n_sub)]
    curve_ids = [(upper * n_half + (place + o) % n_half, sub) for o in range(1, n_half)]
    chain = [(1, me < total - 1, me > 0), (-1, me > 0, me < total - 1), (2, me < total - 2, me > 1)]

    barrier = pltpu.get_barrier_semaphore()

    def signal(peer):
        pl.semaphore_signal(barrier, inc=1, device_id=peer, device_id_type=MESH)

    loads = [
        pltpu.make_async_copy(a, b, load_sem.at[k])
        for k, (a, b) in enumerate(
            [
                (coarse, held), (tags_in, tags), (box_x_in, box_x), (courant_in, courant), (joined_in, joined),
                (alone_in, alone), (tables_in, tables),
            ]
        )
    ]
    for load in loads:
        load.start()
    for peer in curve_ids + sub_ids:
        signal(peer)
    expected = jnp.int32(len(curve_ids) + len(sub_ids))
    for step, sends, gets in chain + [(-2, me > 1, me < total - 2)]:
        @pl.when(sends)
        def _(step=step):
            signal(device(me + step))
        expected = expected + jnp.where(gets, 1, 0)

    for load in loads[1:3]:
        load.wait()
    rank_box = [jnp.int32(0)] * boxes
    seen = jnp.int32(0)
    for b in range(boxes):
        on = tags[b] == 1
        for r in range(b + 1):
            rank_box[r] = jnp.where(on & (seen == r), b, rank_box[r])
        seen = seen + jnp.where(on, 1, 0)
    live = seen

    def box_of(rank):
        found = jnp.int32(0)
        for r in range(boxes):
            found = jnp.where(rank == r, rank_box[r], found)
        return found

    tail_box = [box_of(live - 3 + k) for k in range(3)]
    head_box = [rank_box[k] for k in range(3)]
    lane = lax.broadcasted_iota(jnp.int32, (1, 128), 1)
    row = jnp.where(lane == 0, counts[0] - live, jnp.where(lane == 7, live, 0))
    for k in range(3):
        row = jnp.where(lane == 1 + k, box_x[tail_box[k]], row)
        row = jnp.where(lane == 4 + k, box_x[head_box[k]], row)
    rows[place, sub] = row

    loads[0].wait()
    for f in range(fields):
        at, rim, low = 32 * f, 32 * fields + 8 * (f // 2), 4 * (f % 2)
        to_right[at : at + 16, :] = held[tail_box[1], f]
        to_right[at + 16 : at + 32, :] = held[tail_box[2], f]
        to_right[rim + low : rim + low + 4, :] = held[tail_box[0], f, 12:16, :]
        to_second[rim - 32 * fields + low : rim - 32 * fields + low + 4, :] = held[tail_box[2], f, 12:16, :]
        to_left[at : at + 16, :] = held[head_box[0], f]
        to_left[at + 16 : at + 32, :] = held[head_box[1], f]
        to_left[rim + low : rim + low + 4, :] = held[head_box[2], f, 0:4, :]
    pl.semaphore_wait(barrier, expected)

    def copy_to(src, dst, send_sem, recv_sem, peer):
        return pltpu.make_async_remote_copy(
            src_ref=src, dst_ref=dst, send_sem=send_sem, recv_sem=recv_sem, device_id=peer, device_id_type=MESH
        )

    mine, group = rows.at[place, sub], rows.at[place]
    sub_copies = [copy_to(mine, mine, sub_send.at[o], sub_recv.at[o], peer) for o, peer in enumerate(sub_ids)]
    curve_copies = [
        copy_to(group, all_rows.at[place], curve_send.at[o], curve_recv.at[o], peer)
        for o, peer in enumerate(curve_ids)
    ]
    box_ends = [(to_right, from_left), (to_left, from_right), (to_second, from_second)]
    box_copies = []
    side_copies = []
    for k, (step, sends, gets) in enumerate(chain):
        peer = device(jnp.clip(me + step, 0, total - 1))
        box_copies.append(copy_to(*box_ends[k], box_send.at[k], box_recv.at[k], peer))
        side_copies.append(copy_to(mine, side.at[k], side_send.at[k], side_recv.at[k], peer))
    for copy in sub_copies:
        copy.start()
    for k, (step, sends, gets) in enumerate(chain):
        @pl.when(sends)
        def _(k=k):
            side_copies[k].start()
            box_copies[k].start()

    for load in loads[3:]:
        load.wait()
    for f in range(fields):
        taps = step_taps(courant[f])
        both = []
        for s in range(11):
            terms = [taps[m] * taps[s - m] for m in range(6) if 0 <= s - m < 6]
            both.append(functools.reduce(lambda a, b: a + b, terms))
        mat = both[0] * joined[0:fine, :]
        for s in range(1, 11):
            mat = mat + both[s] * joined[s : s + fine, :]
        mats[f, 1] = split_pair(mat)
        one = taps[0] * alone[0:fine, :]
        for s in range(1, 6):
            one = one + taps[s] * alone[s : s + fine, :]
        first_step[0:8, :] = jnp.broadcast_to(one[0:1, :], (8, 128))
        first_step[8 : 8 + fine, :] = one
        first_step[8 + fine : 16 + fine, :] = jnp.broadcast_to(one[fine - 1 : fine, :], (8, 128))
        two = taps[0] * first_step[5 : 5 + fine, :]
        for s in range(1, 6):
            two = two + taps[s] * first_step[5 + s : 5 + s + fine, :]
        mats[f, 0] = split_pair(two)

    top = lax.broadcasted_iota(jnp.int32, (8, 256), 0) < 4
    first_lane = lax.broadcasted_iota(jnp.int32, (fine, 128), 1)

    def across(slot, at, left, own, right, mat):
        data = jnp.concatenate([jnp.where(top, right, left), own], axis=0)
        rest = data - data.astype(jnp.bfloat16).astype(jnp.float32)
        stacked = jnp.concatenate([data, rest], axis=0).astype(jnp.bfloat16)
        stacked = jnp.concatenate([stacked, stacked], axis=0)
        moved = jnp.dot(mat[:, 0:96], stacked, preferred_element_type=jnp.float32)
        a, b = moved[:, 0:128], moved[:, 128:256]
        count = mat.shape[0]
        pick = first_lane[0:count]
        for n, part in enumerate([a, jnp.where(pick < 32, b, a), jnp.where(pick < 96, b, a), b]):
            high = part.astype(jnp.bfloat16)
            windows[slot, n, at : at + count, 0:128] = high
            windows[slot, n, at : at + count, 128:256] = (part - high.astype(jnp.float32)).astype(jnp.bfloat16)

    def spread(slot, f, targets):
        count = sum(n for _, _, n in targets)
        for n in range(4):
            plane = jnp.dot(windows[slot, n, 0:count], tables[n], preferred_element_type=jnp.float32)
            at = 0
            for k, start, size in targets:
                cand[k, f, start : start + size, 256 * n : 256 * n + 256] = plane[at : at + size]
                at += size

    def next_to(a, b):
        return jnp.where(box_x[a] + 1 == box_x[b], 1, 0)

    own = []
    for r in range(boxes):
        before, after = rank_box[max(r - 1, 0)], rank_box[min(r + 1, boxes - 1)]
        left_on = next_to(before, rank_box[r]) if r else jnp.int32(0)
        right_on = jnp.where(r + 1 < live, next_to(rank_box[r], after), 0) if r + 1 < boxes else jnp.int32(0)
        own.append((2 + r, before, rank_box[r], after, left_on, right_on))
    own.append((12, tail_box[1], tail_box[2], tail_box[2], next_to(tail_box[1], tail_box[2]), jnp.int32(0)))

    def inner_x(f):
        for i, (_, before, box, after, left_on, right_on) in enumerate(own):
            mat = jnp.concatenate([mats[f, left_on, 0:16, :], mats[f, right_on, 16:32, :]], axis=0)
            across(f % 2, 32 * i, held[before, f, 8:16, :], held[box, f], held[after, f, 0:8, :], mat)

    def inner_yz(f):
        spread(f % 2, f, [(entry[0], 0, 32) for entry in own])

    early = fields // 2
    inner_x(0)
    for f in range(early):
        if f + 1 < early:
            inner_x(f + 1)
        inner_yz(f)

    for copy in sub_copies:
        copy.wait_recv()
    for copy in curve_copies:
        copy.start()
    keep = pltpu.make_async_copy(group, all_rows.at[place], out_sem.at[0])
    keep.start()

    inner_x(early)
    for f in range(early, fields):
        if f + 1 < fields:
            inner_x(f + 1)
        inner_yz(f)
    cand[13] = jnp.zeros(cand.shape[1:], jnp.float32)

    for k, (step, sends, gets) in enumerate(chain):
        @pl.when(gets)
        def _(k=k):
            side_copies[k].wait_recv()
            box_copies[k].wait_recv()
    right_row, left_row, second_row = side[1], side[0], side[2]
    left_x = [jnp.sum(jnp.where(lane == 1 + k, left_row, 0)) for k in range(3)]
    short = jnp.sum(jnp.where(lane == 7, left_row, 0)) < 3
    left_x[0] = jnp.where(short, jnp.sum(jnp.where(lane == 3, second_row, 0)), left_x[0])
    right_x = [jnp.sum(jnp.where(lane == 4 + k, right_row, 0)) for k in range(3)]

    def joins(a, b, there):
        return jnp.where(there & (a + 1 == b), 1, 0)

    low, high = me > 0, me < total - 1
    low_rim = joins(left_x[0], left_x[1], low)
    low_pair = joins(left_x[1], left_x[2], low)
    low_own = joins(left_x[2], box_x[head_box[0]], low)
    high_own = joins(box_x[tail_box[2]], right_x[0], high)
    high_pair = joins(right_x[0], right_x[1], high)
    high_rim = joins(right_x[1], right_x[2], high)

    def outer_x(f):
        slot, at, rim = f % 2, 32 * f, 32 * fields + 8 * (f // 2)
        left_rim = jnp.where(short, from_second[rim - 32 * fields : rim - 32 * fields + 8, :], from_left[rim : rim + 8, :])
        right_rim = from_right[rim : rim + 8, :]
        if f % 2 == 0:
            left_rim = pltpu.roll(left_rim, 4, 0)
        else:
            right_rim = pltpu.roll(right_rim, 4, 0)
        zero = jnp.zeros((8, 256), jnp.float32)
        head, tail = held[head_box[0], f, 0:8, :], held[tail_box[2], f, 8:16, :]

        def both(a, b):
            return jnp.concatenate([mats[f, a, 0:16, :], mats[f, b, 16:32, :]], axis=0)

        across(slot, 0, left_rim, from_left[at : at + 16, :], from_left[at + 16 : at + 24, :], both(low_rim, low_pair))
        across(slot, 32, from_left[at + 8 : at + 16, :], from_left[at + 16 : at + 32, :], head, both(low_pair, low_own))
        edge = jnp.where(low_own == 1, from_left[at + 24 : at + 32, :], zero)
        across(slot, 64, edge, held[head_box[0], f], held[head_box[0], f, 8:16, :], mats[f, low_own, 0:16, :])
        edge = jnp.where(high_own == 1, from_right[at : at + 8, :], zero)
        across(slot, 80, held[tail_box[2], f, 0:8, :], held[tail_box[2], f], edge, mats[f, high_own, 16:32, :])
        across(slot, 96, tail, from_right[at : at + 16, :], from_right[at + 16 : at + 24, :], both(high_own, high_pair))
        across(slot, 128, from_right[at + 8 : at + 16, :], from_right[at + 16 : at + 32, :], right_rim, both(high_pair, high_rim))

    def outer_yz(f):
        spread(f % 2, f, [(0, 0, 32), (1, 0, 32), (2, 0, 16), (12, 16, 16), (10, 0, 32), (11, 0, 32)])

    outer_x(0)
    for f in range(fields):
        if f + 1 < fields:
            outer_x(f + 1)
        outer_yz(f)

    keep.wait()
    for copy in curve_copies:
        copy.wait_recv()
    for copy in sub_copies + curve_copies:
        copy.wait_send()
    for k, (step, sends, gets) in enumerate(chain):
        @pl.when(sends)
        def _(k=k):
            side_copies[k].wait_send()
            box_copies[k].wait_send()


def settle(n_curve, n_sub, all_rows, cand, out, sems):
    boxes = out.shape[0]
    n_half = n_curve // 2
    curve, sub = lax.axis_index("curve"), lax.axis_index("sub")
    shape = all_rows.shape
    order = lax.broadcasted_iota(jnp.int32, shape, 0)
    lanes = lax.broadcasted_iota(jnp.int32, shape, 1)
    spot = (curve % n_half) * n_sub + sub
    rows = all_rows[...]
    below = jnp.where((lanes == 0) & (order < spot), rows, 0)
    above = jnp.where((lanes == 0) & (order >= spot), rows, 0)
    offset = jnp.sum(jnp.where(curve < n_half, below, -above))
    change = jnp.sum(jnp.where((lanes == 0) & (order == spot), rows, 0))
    live = jnp.sum(jnp.where((lanes == 7) & (order == spot), rows, 0))
    copies = []
    for j in range(boxes):
        rank = offset + j
        pick = jnp.where(rank < live - 1, 2 + rank, jnp.where(rank == live - 1, 12, 10 + rank - live))
        pick = jnp.clip(jnp.where(j < live + change, pick, 13), 0, 13)
        copy = pltpu.make_async_copy(cand.at[pick], out.at[j], sems.at[j])
        copy.start()
        copies.append(copy)
    for copy in copies:
        copy.wait()


def local(n_curve, n_sub, coarse, tags, box_x, counts, courant):
    boxes, fields, half, plane = coarse.shape
    fine = 2 * half
    joined, alone = x_tables(half)
    tables = jnp.asarray(plane_tables(half), jnp.bfloat16)
    vmem = pl.BlockSpec(memory_space=pltpu.VMEM)
    anywhere = pl.BlockSpec(memory_space=pl.ANY)
    stay = pl.BlockSpec(memory_space=pltpu.HBM)
    packed = 36 * fields
    dma = pltpu.SemaphoreType.DMA
    n_half = n_curve // 2
    edge = pltpu.VMEM((packed, plane), jnp.float32)
    rim = pltpu.VMEM((4 * fields, plane), jnp.float32)
    inputs = (tags, box_x, courant, coarse, jnp.asarray(joined), jnp.asarray(alone), tables)
    all_rows, cand = pl.pallas_call(
        functools.partial(exchange, n_curve, n_sub),
        out_shape=(
            jax.ShapeDtypeStruct((n_half, n_sub, 1, 128), jnp.int32),
            jax.ShapeDtypeStruct((boxes + 6, fields, fine, 4 * plane), jnp.float32),
        ),
        in_specs=[stay] * 7 + [pl.BlockSpec(memory_space=pltpu.SMEM)],
        out_specs=(vmem, vmem),
        scratch_shapes=[
            pltpu.SMEM((boxes,), jnp.int32),
            pltpu.SMEM((boxes,), jnp.int32),
            pltpu.SMEM((fields,), jnp.float32),
            pltpu.VMEM((48, 128), jnp.float32),
            pltpu.VMEM((40, 128), jnp.float32),
            pltpu.VMEM(tables.shape, jnp.bfloat16),
            pltpu.VMEM((fields, 2, fine, 128), jnp.bfloat16),
            pltpu.VMEM((2, 4, (boxes + 1) * fine, plane), jnp.bfloat16),
            pltpu.VMEM(coarse.shape, jnp.float32),
            edge, edge, rim,
            edge, edge, rim,
            pltpu.VMEM((n_half, n_sub, 1, 128), jnp.int32),
            pltpu.VMEM((3, 1, 128), jnp.int32),
            pltpu.VMEM((48, 128), jnp.float32),
            dma((7,)),
            dma((1,)),
            dma((3,)),
            dma((3,)),
            dma((3,)),
            dma((3,)),
            dma((n_sub - 1,)),
            dma((n_sub - 1,)),
            dma((n_half - 1,)),
            dma((n_half - 1,)),
        ],
        compiler_params=pltpu.CompilerParams(collective_id=0, has_side_effects=True, vmem_limit_bytes=24 * 2**20),
        name="exchange",
    )(*[pltpu.with_memory_space_constraint(a, pltpu.HBM) for a in inputs], counts)
    return pl.pallas_call(
        functools.partial(settle, n_curve, n_sub),
        out_shape=jax.ShapeDtypeStruct((boxes, fields, fine, 4 * plane), jnp.float32),
        in_specs=[vmem, vmem],
        out_specs=anywhere,
        scratch_shapes=[dma((boxes,))],
        compiler_params=pltpu.CompilerParams(vmem_limit_bytes=16 * 2**20),
        name="settle",
    )(all_rows.reshape(n_half * n_sub, 128), cand)


def solution(mesh):
    both = ("curve", "sub")
    in_specs = (P(both, None, None, None), P(both), P(both), P(both), P())
    return jax.shard_map(
        functools.partial(local, mesh.shape["curve"], mesh.shape["sub"]),
        mesh=mesh,
        in_specs=in_specs,
        out_specs=P(both, None, None, None),
        check_vma=False,
    )
```

```python
import functools

import jax
import jax.numpy as jnp
import numpy as np
from jax import lax
from jax.experimental import pallas as pl
from jax.experimental.pallas import tpu as pltpu
from jax.sharding import PartitionSpec as P

MESH = pl.DeviceIdType.MESH
MOVE = 2
LEFT_REACH, RIGHT_REACH = 3, 2


def line_table(coarse_len):
    table = np.zeros((2 * coarse_len, coarse_len), np.float64)
    for cell in range(2 * coarse_len):
        i, sign = cell // 2, (-0.25 if cell % 2 == 0 else 0.25)
        ahead, behind = min(i + 1, coarse_len - 1), max(i - 1, 0)
        table[cell, i] += 1.0
        table[cell, ahead] += sign / (ahead - behind)
        table[cell, behind] -= sign / (ahead - behind)
    return table


def x_tables(half):
    line = line_table(half)
    fine = 2 * half
    wide = np.zeros((3 * fine, 3 * half))
    for box in range(3):
        wide[box * fine : (box + 1) * fine, box * half : (box + 1) * half] = line
    cols = np.concatenate([2 * half + np.arange(4), half - 4 + np.arange(4), half + np.arange(half)])
    joined = wide[fine - 2 * LEFT_REACH : 2 * fine + 2 * RIGHT_REACH, cols]
    alone = np.concatenate(
        [wide[fine : fine + 1]] * LEFT_REACH + [wide[fine : 2 * fine]] + [wide[2 * fine - 1 : 2 * fine]] * RIGHT_REACH
    )[:, cols]

    def grow(a, rows):
        a = np.tile(np.pad(a, ((0, rows - a.shape[0]), (0, 0))), (1, 4))
        return np.pad(a, ((0, 0), (0, 128 - a.shape[1]))).astype(np.float32)

    return grow(joined, 48), grow(alone, 40)


def plane_tables(half):
    line = line_table(half)
    table = np.kron(line, line).T
    size = half * half
    lane = np.arange(size // 2)
    picks = [lane, np.where(lane < 32, lane + 128, lane), np.where(lane < 96, lane + 128, lane), lane + 128]
    quarters = []
    for n, pick in enumerate(picks):
        columns = table[:, n * size : (n + 1) * size]
        missed = np.delete(columns, pick, axis=0)
        assert not missed.any()
        quarters.append(np.concatenate([columns[pick], columns[pick]]))
    return np.stack(quarters)


def step_taps(c):
    c2 = c * c
    c3 = c2 * c
    right, left, own = c - 2.0 * c2 + c3, c3 - c2, 3.0 * c2 - 2.0 * c3
    t = 1.0 / 12.0
    flux = (
        -t * left,
        7.0 * t * left - t * right,
        7.0 * t * (left + right) + own,
        7.0 * t * right - t * left,
        -t * right,
    )
    return (
        flux[0],
        flux[1] - flux[0],
        flux[2] - flux[1],
        1.0 + flux[3] - flux[2],
        flux[4] - flux[3],
        -flux[4],
    )


def split_pair(mat):
    high = mat.astype(jnp.bfloat16).astype(jnp.float32)
    lane = lax.broadcasted_iota(jnp.int32, mat.shape, 1)
    return jnp.where(lane < 48, high, mat - high).astype(jnp.bfloat16)


def exchange(
    n_curve, n_sub,
    tags_in, box_x_in, courant_in, coarse, joined_in, alone_in, tables_in, counts,
    all_rows, cand,
    tags, box_x, courant, joined, alone, tables, mats, windows,
    held, to_right, to_left, to_second, from_left, from_right, from_second, rows, side, first_step,
    load_sem, out_sem, box_send, box_recv, side_send, side_recv, sub_send, sub_recv, curve_send, curve_recv,
):
    boxes = coarse.shape[0]
    fields = coarse.shape[1]
    fine = 32
    n_half = n_curve // 2
    curve, sub = lax.axis_index("curve"), lax.axis_index("sub")
    me = curve * n_sub + sub
    total = n_curve * n_sub
    upper = curve // n_half
    place = curve % n_half

    def device(index):
        return (index // n_sub, index % n_sub)

    sub_ids = [(curve, (sub + o) % n_sub) for o in range(1, n_sub)]
    curve_ids = [(upper * n_half + (place + o) % n_half, sub) for o in range(1, n_half)]
    chain = [(1, me < total - 1, me > 0), (-1, me > 0, me < total - 1), (2, me < total - 2, me > 1)]

    barrier = pltpu.get_barrier_semaphore()

    def signal(peer):
        pl.semaphore_signal(barrier, inc=1, device_id=peer, device_id_type=MESH)

    loads = [
        pltpu.make_async_copy(a, b, load_sem.at[k])
        for k, (a, b) in enumerate(
            [
                (coarse, held), (tags_in, tags), (box_x_in, box_x), (courant_in, courant), (joined_in, joined),
                (alone_in, alone), (tables_in, tables),
            ]
        )
    ]
    for load in loads:
        load.start()
    goes = [jnp.where(upper == 0, place + o < n_half, place + o >= n_half) for o in range(1, n_half)]
    comes = [jnp.where(upper == 0, place - o >= 0, place - o < 0) for o in range(1, n_half)]
    for o in range(1, n_half):
        @pl.when(comes[o - 1])
        def _(o=o):
            signal((upper * n_half + (place - o + n_half) % n_half, sub))
    for peer in sub_ids:
        signal(peer)
    expected = jnp.int32(len(sub_ids)) + jnp.where(upper == 0, n_half - 1 - place, place)
    for step, sends, gets in chain:
        @pl.when(gets)
        def _(step=step):
            signal(device(me - step))
        expected = expected + jnp.where(sends, 1, 0)

    for load in loads[1:3]:
        load.wait()
    rank_box = [jnp.int32(0)] * boxes
    seen = jnp.int32(0)
    for b in range(boxes):
        on = tags[b] == 1
        for r in range(b + 1):
            rank_box[r] = jnp.where(on & (seen == r), b, rank_box[r])
        seen = seen + jnp.where(on, 1, 0)
    live = seen

    def box_of(rank):
        found = jnp.int32(0)
        for r in range(boxes):
            found = jnp.where(rank == r, rank_box[r], found)
        return found

    tail_box = [box_of(live - 3 + k) for k in range(3)]
    head_box = [rank_box[k] for k in range(3)]
    lane = lax.broadcasted_iota(jnp.int32, (1, 128), 1)
    row = jnp.where(lane == 0, counts[0] - live, jnp.where(lane == 7, live, 0))
    for k in range(3):
        row = jnp.where(lane == 1 + k, box_x[tail_box[k]], row)
        row = jnp.where(lane == 4 + k, box_x[head_box[k]], row)
    rows[place, sub] = row

    loads[0].wait()
    for f in range(fields):
        at, rim, low = 32 * f, 32 * fields + 8 * (f // 2), 4 * (f % 2)
        to_right[at : at + 16, :] = held[tail_box[1], f]
        to_right[at + 16 : at + 32, :] = held[tail_box[2], f]
        to_right[rim + low : rim + low + 4, :] = held[tail_box[0], f, 12:16, :]
        to_second[rim - 32 * fields + low : rim - 32 * fields + low + 4, :] = held[tail_box[2], f, 12:16, :]
        to_left[at : at + 16, :] = held[head_box[0], f]
        to_left[at + 16 : at + 32, :] = held[head_box[1], f]
        to_left[rim + low : rim + low + 4, :] = held[head_box[2], f, 0:4, :]
    pl.semaphore_wait(barrier, expected)

    def copy_to(src, dst, send_sem, recv_sem, peer):
        return pltpu.make_async_remote_copy(
            src_ref=src, dst_ref=dst, send_sem=send_sem, recv_sem=recv_sem, device_id=peer, device_id_type=MESH
        )

    mine, group = rows.at[place, sub], rows.at[place]
    sub_copies = [copy_to(mine, mine, sub_send.at[o], sub_recv.at[o], peer) for o, peer in enumerate(sub_ids)]
    curve_copies = [
        copy_to(group, all_rows.at[place], curve_send.at[o], curve_recv.at[o], peer)
        for o, peer in enumerate(curve_ids)
    ]
    box_ends = [(to_right, from_left), (to_left, from_right), (to_second, from_second)]
    box_copies = []
    side_copies = []
    for k, (step, sends, gets) in enumerate(chain):
        peer = device(jnp.clip(me + step, 0, total - 1))
        box_copies.append(copy_to(*box_ends[k], box_send.at[k], box_recv.at[k], peer))
        side_copies.append(copy_to(mine, side.at[k], side_send.at[k], side_recv.at[k], peer))
    for copy in sub_copies:
        copy.start()
    for k, (step, sends, gets) in enumerate(chain):
        @pl.when(sends)
        def _(k=k):
            side_copies[k].start()
            box_copies[k].start()

    for load in loads[3:]:
        load.wait()
    for f in range(fields):
        taps = step_taps(courant[f])
        both = []
        for s in range(11):
            terms = [taps[m] * taps[s - m] for m in range(6) if 0 <= s - m < 6]
            both.append(functools.reduce(lambda a, b: a + b, terms))
        mat = both[0] * joined[0:fine, :]
        for s in range(1, 11):
            mat = mat + both[s] * joined[s : s + fine, :]
        mats[f, 1] = split_pair(mat)
        one = taps[0] * alone[0:fine, :]
        for s in range(1, 6):
            one = one + taps[s] * alone[s : s + fine, :]
        first_step[0:8, :] = jnp.broadcast_to(one[0:1, :], (8, 128))
        first_step[8 : 8 + fine, :] = one
        first_step[8 + fine : 16 + fine, :] = jnp.broadcast_to(one[fine - 1 : fine, :], (8, 128))
        two = taps[0] * first_step[5 : 5 + fine, :]
        for s in range(1, 6):
            two = two + taps[s] * first_step[5 + s : 5 + s + fine, :]
        mats[f, 0] = split_pair(two)

    top = lax.broadcasted_iota(jnp.int32, (8, 256), 0) < 4
    first_lane = lax.broadcasted_iota(jnp.int32, (fine, 128), 1)

    def across(slot, at, left, own, right, mat):
        data = jnp.concatenate([jnp.where(top, right, left), own], axis=0)
        rest = data - data.astype(jnp.bfloat16).astype(jnp.float32)
        stacked = jnp.concatenate([data, rest], axis=0).astype(jnp.bfloat16)
        stacked = jnp.concatenate([stacked, stacked], axis=0)
        moved = jnp.dot(mat[:, 0:96], stacked, preferred_element_type=jnp.float32)
        a, b = moved[:, 0:128], moved[:, 128:256]
        count = mat.shape[0]
        pick = first_lane[0:count]
        for n, part in enumerate([a, jnp.where(pick < 32, b, a), jnp.where(pick < 96, b, a), b]):
            high = part.astype(jnp.bfloat16)
            windows[slot, n, at : at + count, 0:128] = high
            windows[slot, n, at : at + count, 128:256] = (part - high.astype(jnp.float32)).astype(jnp.bfloat16)

    def spread(slot, f, targets):
        count = sum(n for _, _, n in targets)
        for n in range(4):
            plane = jnp.dot(windows[slot, n, 0:count], tables[n], preferred_element_type=jnp.float32)
            at = 0
            for k, start, size in targets:
                cand[k, f, start : start + size, 256 * n : 256 * n + 256] = plane[at : at + size]
                at += size

    def next_to(a, b):
        return jnp.where(box_x[a] + 1 == box_x[b], 1, 0)

    own = []
    for r in range(boxes):
        before, after = rank_box[max(r - 1, 0)], rank_box[min(r + 1, boxes - 1)]
        left_on = next_to(before, rank_box[r]) if r else jnp.int32(0)
        right_on = jnp.where(r + 1 < live, next_to(rank_box[r], after), 0) if r + 1 < boxes else jnp.int32(0)
        own.append((2 + r, before, rank_box[r], after, left_on, right_on))
    own.append((12, tail_box[1], tail_box[2], tail_box[2], next_to(tail_box[1], tail_box[2]), jnp.int32(0)))

    def inner_x(f):
        for i, (_, before, box, after, left_on, right_on) in enumerate(own):
            mat = jnp.concatenate([mats[f, left_on, 0:16, :], mats[f, right_on, 16:32, :]], axis=0)
            across(f % 2, 32 * i, held[before, f, 8:16, :], held[box, f], held[after, f, 0:8, :], mat)

    def inner_yz(f):
        spread(f % 2, f, [(entry[0], 0, 32) for entry in own])

    early = fields // 2
    inner_x(0)
    for f in range(early):
        if f + 1 < early:
            inner_x(f + 1)
        inner_yz(f)

    for copy in sub_copies:
        copy.wait_recv()
    for o, copy in enumerate(curve_copies):
        pl.when(goes[o])(copy.start)
    keep = pltpu.make_async_copy(group, all_rows.at[place], out_sem.at[0])
    keep.start()

    inner_x(early)
    for f in range(early, fields):
        if f + 1 < fields:
            inner_x(f + 1)
        inner_yz(f)
    cand[13] = jnp.zeros(cand.shape[1:], jnp.float32)

    for k, (step, sends, gets) in enumerate(chain):
        @pl.when(gets)
        def _(k=k):
            side_copies[k].wait_recv()
            box_copies[k].wait_recv()
    right_row, left_row, second_row = side[1], side[0], side[2]
    left_x = [jnp.sum(jnp.where(lane == 1 + k, left_row, 0)) for k in range(3)]
    short = jnp.sum(jnp.where(lane == 7, left_row, 0)) < 3
    left_x[0] = jnp.where(short, jnp.sum(jnp.where(lane == 3, second_row, 0)), left_x[0])
    right_x = [jnp.sum(jnp.where(lane == 4 + k, right_row, 0)) for k in range(3)]

    def joins(a, b, there):
        return jnp.where(there & (a + 1 == b), 1, 0)

    low, high = me > 0, me < total - 1
    low_rim = joins(left_x[0], left_x[1], low)
    low_pair = joins(left_x[1], left_x[2], low)
    low_own = joins(left_x[2], box_x[head_box[0]], low)
    high_own = joins(box_x[tail_box[2]], right_x[0], high)
    high_pair = joins(right_x[0], right_x[1], high)
    high_rim = joins(right_x[1], right_x[2], high)

    def outer_x(f):
        slot, at, rim = f % 2, 32 * f, 32 * fields + 8 * (f // 2)
        left_rim = jnp.where(short, from_second[rim - 32 * fields : rim - 32 * fields + 8, :], from_left[rim : rim + 8, :])
        right_rim = from_right[rim : rim + 8, :]
        if f % 2 == 0:
            left_rim = pltpu.roll(left_rim, 4, 0)
        else:
            right_rim = pltpu.roll(right_rim, 4, 0)
        zero = jnp.zeros((8, 256), jnp.float32)
        head, tail = held[head_box[0], f, 0:8, :], held[tail_box[2], f, 8:16, :]

        def both(a, b):
            return jnp.concatenate([mats[f, a, 0:16, :], mats[f, b, 16:32, :]], axis=0)

        across(slot, 0, left_rim, from_left[at : at + 16, :], from_left[at + 16 : at + 24, :], both(low_rim, low_pair))
        across(slot, 32, from_left[at + 8 : at + 16, :], from_left[at + 16 : at + 32, :], head, both(low_pair, low_own))
        edge = jnp.where(low_own == 1, from_left[at + 24 : at + 32, :], zero)
        across(slot, 64, edge, held[head_box[0], f], held[head_box[0], f, 8:16, :], mats[f, low_own, 0:16, :])
        edge = jnp.where(high_own == 1, from_right[at : at + 8, :], zero)
        across(slot, 80, held[tail_box[2], f, 0:8, :], held[tail_box[2], f], edge, mats[f, high_own, 16:32, :])
        across(slot, 96, tail, from_right[at : at + 16, :], from_right[at + 16 : at + 24, :], both(high_own, high_pair))
        across(slot, 128, from_right[at + 8 : at + 16, :], from_right[at + 16 : at + 32, :], right_rim, both(high_pair, high_rim))

    def outer_yz(f):
        spread(f % 2, f, [(0, 0, 32), (1, 0, 32), (2, 0, 16), (12, 16, 16), (10, 0, 32), (11, 0, 32)])

    outer_x(0)
    for f in range(fields):
        if f + 1 < fields:
            outer_x(f + 1)
        outer_yz(f)

    keep.wait()
    for o, copy in enumerate(curve_copies):
        pl.when(comes[o])(copy.wait_recv)
    for copy in sub_copies:
        copy.wait_send()
    for o, copy in enumerate(curve_copies):
        pl.when(goes[o])(copy.wait_send)
    for k, (step, sends, gets) in enumerate(chain):
        @pl.when(sends)
        def _(k=k):
            side_copies[k].wait_send()
            box_copies[k].wait_send()


def settle(n_curve, n_sub, all_rows, cand, out, sems):
    boxes = out.shape[0]
    n_half = n_curve // 2
    curve, sub = lax.axis_index("curve"), lax.axis_index("sub")
    shape = all_rows.shape
    order = lax.broadcasted_iota(jnp.int32, shape, 0)
    lanes = lax.broadcasted_iota(jnp.int32, shape, 1)
    spot = (curve % n_half) * n_sub + sub
    rows = all_rows[...]
    below = jnp.where((lanes == 0) & (order < spot), rows, 0)
    above = jnp.where((lanes == 0) & (order >= spot), rows, 0)
    offset = jnp.sum(jnp.where(curve < n_half, below, -above))
    change = jnp.sum(jnp.where((lanes == 0) & (order == spot), rows, 0))
    live = jnp.sum(jnp.where((lanes == 7) & (order == spot), rows, 0))
    copies = []
    for j in range(boxes):
        rank = offset + j
        pick = jnp.where(rank < live - 1, 2 + rank, jnp.where(rank == live - 1, 12, 10 + rank - live))
        pick = jnp.clip(jnp.where(j < live + change, pick, 13), 0, 13)
        copy = pltpu.make_async_copy(cand.at[pick], out.at[j], sems.at[j])
        copy.start()
        copies.append(copy)
    for copy in copies:
        copy.wait()


def local(n_curve, n_sub, coarse, tags, box_x, counts, courant):
    boxes, fields, half, plane = coarse.shape
    fine = 2 * half
    joined, alone = x_tables(half)
    tables = jnp.asarray(plane_tables(half), jnp.bfloat16)
    vmem = pl.BlockSpec(memory_space=pltpu.VMEM)
    anywhere = pl.BlockSpec(memory_space=pl.ANY)
    stay = pl.BlockSpec(memory_space=pltpu.HBM)
    packed = 36 * fields
    dma = pltpu.SemaphoreType.DMA
    n_half = n_curve // 2
    edge = pltpu.VMEM((packed, plane), jnp.float32)
    rim = pltpu.VMEM((4 * fields, plane), jnp.float32)
    inputs = (tags, box_x, courant, coarse, jnp.asarray(joined), jnp.asarray(alone), tables)
    all_rows, cand = pl.pallas_call(
        functools.partial(exchange, n_curve, n_sub),
        out_shape=(
            jax.ShapeDtypeStruct((n_half, n_sub, 1, 128), jnp.int32),
            jax.ShapeDtypeStruct((boxes + 6, fields, fine, 4 * plane), jnp.float32),
        ),
        in_specs=[stay] * 7 + [pl.BlockSpec(memory_space=pltpu.SMEM)],
        out_specs=(vmem, vmem),
        scratch_shapes=[
            pltpu.SMEM((boxes,), jnp.int32),
            pltpu.SMEM((boxes,), jnp.int32),
            pltpu.SMEM((fields,), jnp.float32),
            pltpu.VMEM((48, 128), jnp.float32),
            pltpu.VMEM((40, 128), jnp.float32),
            pltpu.VMEM(tables.shape, jnp.bfloat16),
            pltpu.VMEM((fields, 2, fine, 128), jnp.bfloat16),
            pltpu.VMEM((2, 4, (boxes + 1) * fine, plane), jnp.bfloat16),
            pltpu.VMEM(coarse.shape, jnp.float32),
            edge, edge, rim,
            edge, edge, rim,
            pltpu.VMEM((n_half, n_sub, 1, 128), jnp.int32),
            pltpu.VMEM((3, 1, 128), jnp.int32),
            pltpu.VMEM((48, 128), jnp.float32),
            dma((7,)),
            dma((1,)),
            dma((3,)),
            dma((3,)),
            dma((3,)),
            dma((3,)),
            dma((n_sub - 1,)),
            dma((n_sub - 1,)),
            dma((n_half - 1,)),
            dma((n_half - 1,)),
        ],
        compiler_params=pltpu.CompilerParams(collective_id=0, has_side_effects=True, vmem_limit_bytes=24 * 2**20),
        name="exchange",
    )(*[pltpu.with_memory_space_constraint(a, pltpu.HBM) for a in inputs], counts)
    return pl.pallas_call(
        functools.partial(settle, n_curve, n_sub),
        out_shape=jax.ShapeDtypeStruct((boxes, fields, fine, 4 * plane), jnp.float32),
        in_specs=[vmem, vmem],
        out_specs=anywhere,
        scratch_shapes=[dma((boxes,))],
        compiler_params=pltpu.CompilerParams(vmem_limit_bytes=16 * 2**20),
        name="settle",
    )(all_rows.reshape(n_half * n_sub, 128), cand)


def solution(mesh):
    both = ("curve", "sub")
    in_specs = (P(both, None, None, None), P(both), P(both), P(both), P())
    return jax.shard_map(
        functools.partial(local, mesh.shape["curve"], mesh.shape["sub"]),
        mesh=mesh,
        in_specs=in_specs,
        out_specs=P(both, None, None, None),
        check_vma=False,
    )
```

```python
import functools

import jax
import jax.numpy as jnp
import numpy as np
from jax import lax
from jax.experimental import pallas as pl
from jax.experimental.pallas import tpu as pltpu
from jax.sharding import PartitionSpec as P

MESH = pl.DeviceIdType.MESH
MOVE = 2
LEFT_REACH, RIGHT_REACH = 3, 2


def line_table(coarse_len):
    table = np.zeros((2 * coarse_len, coarse_len), np.float64)
    for cell in range(2 * coarse_len):
        i, sign = cell // 2, (-0.25 if cell % 2 == 0 else 0.25)
        ahead, behind = min(i + 1, coarse_len - 1), max(i - 1, 0)
        table[cell, i] += 1.0
        table[cell, ahead] += sign / (ahead - behind)
        table[cell, behind] -= sign / (ahead - behind)
    return table


def x_tables(half):
    line = line_table(half)
    fine = 2 * half
    wide = np.zeros((3 * fine, 3 * half))
    for box in range(3):
        wide[box * fine : (box + 1) * fine, box * half : (box + 1) * half] = line
    cols = np.concatenate([2 * half + np.arange(4), half - 4 + np.arange(4), half + np.arange(half)])
    joined = wide[fine - 2 * LEFT_REACH : 2 * fine + 2 * RIGHT_REACH, cols]
    alone = np.concatenate(
        [wide[fine : fine + 1]] * LEFT_REACH + [wide[fine : 2 * fine]] + [wide[2 * fine - 1 : 2 * fine]] * RIGHT_REACH
    )[:, cols]

    def grow(a, rows):
        a = np.tile(np.pad(a, ((0, rows - a.shape[0]), (0, 0))), (1, 4))
        return np.pad(a, ((0, 0), (0, 128 - a.shape[1]))).astype(np.float32)

    return grow(joined, 48), grow(alone, 40)


def plane_tables(half):
    line = line_table(half)
    table = np.kron(line, line).T
    size = half * half
    lane = np.arange(size // 2)
    picks = [lane, np.where(lane < 32, lane + 128, lane), np.where(lane < 96, lane + 128, lane), lane + 128]
    quarters = []
    for n, pick in enumerate(picks):
        columns = table[:, n * size : (n + 1) * size]
        missed = np.delete(columns, pick, axis=0)
        assert not missed.any()
        quarters.append(np.concatenate([columns[pick], columns[pick]]))
    return np.stack(quarters)


def step_taps(c):
    c2 = c * c
    c3 = c2 * c
    right, left, own = c - 2.0 * c2 + c3, c3 - c2, 3.0 * c2 - 2.0 * c3
    t = 1.0 / 12.0
    flux = (
        -t * left,
        7.0 * t * left - t * right,
        7.0 * t * (left + right) + own,
        7.0 * t * right - t * left,
        -t * right,
    )
    return (
        flux[0],
        flux[1] - flux[0],
        flux[2] - flux[1],
        1.0 + flux[3] - flux[2],
        flux[4] - flux[3],
        -flux[4],
    )


def split_pair(mat):
    high = mat.astype(jnp.bfloat16).astype(jnp.float32)
    lane = lax.broadcasted_iota(jnp.int32, mat.shape, 1)
    return jnp.where(lane < 48, high, mat - high).astype(jnp.bfloat16)


def exchange(
    n_curve, n_sub,
    tags_in, box_x_in, courant_in, coarse, joined_in, alone_in, tables_in, counts,
    all_rows, cand,
    tags, box_x, courant, joined, alone, tables, mats, windows,
    held, to_right, to_left, to_second, from_left, from_right, from_second, rows, beside, first_step,
    load_sem, out_sem, box_send, box_recv, side_send, side_recv, sub_send, sub_recv, curve_send, curve_recv,
):
    boxes = coarse.shape[0]
    fields = coarse.shape[1]
    fine = 32
    n_half = n_curve // 2
    curve, sub = lax.axis_index("curve"), lax.axis_index("sub")
    me = curve * n_sub + sub
    total = n_curve * n_sub
    upper = curve // n_half
    place = curve % n_half

    def device(index):
        return (index // n_sub, index % n_sub)

    sub_ids = [(curve, (sub + o) % n_sub) for o in range(1, n_sub)]
    curve_ids = [(upper * n_half + (place + o) % n_half, sub) for o in range(1, n_half)]
    chain = [(1, me < total - 1, me > 0), (-1, me > 0, me < total - 1), (2, me < total - 2, me > 1)]

    barrier = pltpu.get_barrier_semaphore()

    def signal(peer):
        pl.semaphore_signal(barrier, inc=1, device_id=peer, device_id_type=MESH)

    loads = [
        pltpu.make_async_copy(a, b, load_sem.at[k])
        for k, (a, b) in enumerate(
            [
                (coarse, held), (tags_in, tags), (box_x_in, box_x), (courant_in, courant), (joined_in, joined),
                (alone_in, alone), (tables_in, tables),
            ]
        )
    ]
    for load in loads:
        load.start()
    goes = [jnp.where(upper == 0, place + o < n_half, place + o >= n_half) for o in range(1, n_half)]
    comes = [jnp.where(upper == 0, place - o >= 0, place - o < 0) for o in range(1, n_half)]
    for o in range(1, n_half):
        @pl.when(comes[o - 1])
        def _(o=o):
            signal((upper * n_half + (place - o + n_half) % n_half, sub))
    for peer in sub_ids:
        signal(peer)
    expected = jnp.int32(len(sub_ids)) + jnp.where(upper == 0, n_half - 1 - place, place)
    for step, sends, gets in chain:
        @pl.when(gets)
        def _(step=step):
            signal(device(me - step))
        expected = expected + jnp.where(sends, 1, 0)

    for load in loads[1:3]:
        load.wait()
    rank_box = [jnp.int32(0)] * boxes
    seen = jnp.int32(0)
    for b in range(boxes):
        on = tags[b] == 1
        for r in range(b + 1):
            rank_box[r] = jnp.where(on & (seen == r), b, rank_box[r])
        seen = seen + jnp.where(on, 1, 0)
    live = seen

    def box_of(rank):
        found = jnp.int32(0)
        for r in range(boxes):
            found = jnp.where(rank == r, rank_box[r], found)
        return found

    tail_box = [box_of(live - 3 + k) for k in range(3)]
    head_box = [rank_box[k] for k in range(3)]
    lane = lax.broadcasted_iota(jnp.int32, (1, 128), 1)
    row = jnp.where(lane == 0, counts[0] - live, jnp.where(lane == 7, live, 0))
    for k in range(3):
        row = jnp.where(lane == 1 + k, box_x[tail_box[k]], row)
        row = jnp.where(lane == 4 + k, box_x[head_box[k]], row)
    rows[place, sub] = row

    loads[0].wait()
    for f in range(fields):
        at, rim, low = 32 * f, 32 * fields + 8 * (f // 2), 4 * (f % 2)
        to_right[at : at + 16, :] = held[tail_box[1], f]
        to_right[at + 16 : at + 32, :] = held[tail_box[2], f]
        to_right[rim + low : rim + low + 4, :] = held[tail_box[0], f, 12:16, :]
        to_second[rim - 32 * fields + low : rim - 32 * fields + low + 4, :] = held[tail_box[2], f, 12:16, :]
        to_left[at : at + 16, :] = held[head_box[0], f]
        to_left[at + 16 : at + 32, :] = held[head_box[1], f]
        to_left[rim + low : rim + low + 4, :] = held[head_box[2], f, 0:4, :]
    for load in loads[3:]:
        load.wait()
    for f in range(fields):
        taps = step_taps(courant[f])
        both = []
        for s in range(11):
            terms = [taps[m] * taps[s - m] for m in range(6) if 0 <= s - m < 6]
            both.append(functools.reduce(lambda a, b: a + b, terms))
        mat = both[0] * joined[0:fine, :]
        for s in range(1, 11):
            mat = mat + both[s] * joined[s : s + fine, :]
        mats[f, 1] = split_pair(mat)
        one = taps[0] * alone[0:fine, :]
        for s in range(1, 6):
            one = one + taps[s] * alone[s : s + fine, :]
        first_step[0:8, :] = jnp.broadcast_to(one[0:1, :], (8, 128))
        first_step[8 : 8 + fine, :] = one
        first_step[8 + fine : 16 + fine, :] = jnp.broadcast_to(one[fine - 1 : fine, :], (8, 128))
        two = taps[0] * first_step[5 : 5 + fine, :]
        for s in range(1, 6):
            two = two + taps[s] * first_step[5 + s : 5 + s + fine, :]
        mats[f, 0] = split_pair(two)

    top = lax.broadcasted_iota(jnp.int32, (8, 256), 0) < 4
    first_lane = lax.broadcasted_iota(jnp.int32, (fine, 128), 1)

    def across(slot, at, left, own, right, mat):
        data = jnp.concatenate([jnp.where(top, right, left), own], axis=0)
        rest = data - data.astype(jnp.bfloat16).astype(jnp.float32)
        stacked = jnp.concatenate([data, rest], axis=0).astype(jnp.bfloat16)
        stacked = jnp.concatenate([stacked, stacked], axis=0)
        moved = jnp.dot(mat[:, 0:96], stacked, preferred_element_type=jnp.float32)
        a, b = moved[:, 0:128], moved[:, 128:256]
        count = mat.shape[0]
        pick = first_lane[0:count]
        for n, part in enumerate([a, jnp.where(pick < 32, b, a), jnp.where(pick < 96, b, a), b]):
            high = part.astype(jnp.bfloat16)
            windows[slot, n, at : at + count, 0:128] = high
            windows[slot, n, at : at + count, 128:256] = (part - high.astype(jnp.float32)).astype(jnp.bfloat16)

    def spread(slot, f, targets):
        count = sum(n for _, _, n in targets)
        for n in range(4):
            plane = jnp.dot(windows[slot, n, 0:count], tables[n], preferred_element_type=jnp.float32)
            at = 0
            for k, start, size in targets:
                cand[k, f, start : start + size, 256 * n : 256 * n + 256] = plane[at : at + size]
                at += size

    def next_to(a, b):
        return jnp.where(box_x[a] + 1 == box_x[b], 1, 0)

    own = []
    for r in range(boxes):
        before, after = rank_box[max(r - 1, 0)], rank_box[min(r + 1, boxes - 1)]
        left_on = next_to(before, rank_box[r]) if r else jnp.int32(0)
        right_on = jnp.where(r + 1 < live, next_to(rank_box[r], after), 0) if r + 1 < boxes else jnp.int32(0)
        own.append((2 + r, before, rank_box[r], after, left_on, right_on))
    own.append((12, tail_box[1], tail_box[2], tail_box[2], next_to(tail_box[1], tail_box[2]), jnp.int32(0)))

    def inner(h, carry):
        count = fields // 2

        def inner_x(k):
            f = count * h + k
            for i, (_, before, box, after, left_on, right_on) in enumerate(own):
                mat = jnp.concatenate([mats[f, left_on, 0:16, :], mats[f, right_on, 16:32, :]], axis=0)
                across(k % 2, 32 * i, held[before, f, 8:16, :], held[box, f], held[after, f, 0:8, :], mat)

        inner_x(0)
        for k in range(count):
            if k + 1 < count:
                inner_x(k + 1)
            spread(k % 2, count * h + k, [(entry[0], 0, 32) for entry in own])
        return carry

    row_y, chip_x = curve % 4, sub // 2
    done = jnp.where(chip_x + row_y == 0, 2, jnp.where((row_y == 0) | (chip_x == 0), 1, 0))
    then = jnp.minimum(done + 1, 2)
    lax.fori_loop(0, done, inner, 0)
    pl.semaphore_wait(barrier, expected)

    def copy_to(src, dst, send_sem, recv_sem, peer):
        return pltpu.make_async_remote_copy(
            src_ref=src, dst_ref=dst, send_sem=send_sem, recv_sem=recv_sem, device_id=peer, device_id_type=MESH
        )

    mine, group = rows.at[place, sub], rows.at[place]
    sub_copies = [copy_to(mine, mine, sub_send.at[o], sub_recv.at[o], peer) for o, peer in enumerate(sub_ids)]
    curve_copies = [
        copy_to(group, all_rows.at[place], curve_send.at[o], curve_recv.at[o], peer)
        for o, peer in enumerate(curve_ids)
    ]
    box_ends = [(to_right, from_left), (to_left, from_right), (to_second, from_second)]
    box_copies = []
    side_copies = []
    for k, (step, sends, gets) in enumerate(chain):
        peer = device(jnp.clip(me + step, 0, total - 1))
        box_copies.append(copy_to(*box_ends[k], box_send.at[k], box_recv.at[k], peer))
        side_copies.append(copy_to(mine, beside.at[k], side_send.at[k], side_recv.at[k], peer))
    for copy in sub_copies:
        copy.start()
    for k, (step, sends, gets) in enumerate(chain):
        @pl.when(sends)
        def _(k=k):
            side_copies[k].start()
            box_copies[k].start()

    lax.fori_loop(done, then, inner, 0)

    for copy in sub_copies:
        copy.wait_recv()
    for o, copy in enumerate(curve_copies):
        pl.when(goes[o])(copy.start)
    keep = pltpu.make_async_copy(group, all_rows.at[place], out_sem.at[0])
    keep.start()

    lax.fori_loop(then, 2, inner, 0)
    cand[13] = jnp.zeros(cand.shape[1:], jnp.float32)

    def arrive(which):
        for k in which:
            @pl.when(chain[k][2])
            def _(k=k):
                side_copies[k].wait_recv()
                box_copies[k].wait_recv()

    def joins(a, b, there):
        return jnp.where(there & (a + 1 == b), 1, 0)

    def pair(f, a, b):
        return jnp.concatenate([mats[f, a, 0:16, :], mats[f, b, 16:32, :]], axis=0)

    zero = jnp.zeros((8, 256), jnp.float32)

    def in_turn(x_part, targets):
        x_part(0)
        for f in range(fields):
            if f + 1 < fields:
                x_part(f + 1)
            spread(f % 2, f, targets)

    def left_joins(whole):
        left_row = beside[0]
        low = me > 0
        left_x = [jnp.sum(jnp.where(lane == 1 + k, left_row, 0)) for k in range(3)]
        low_pair = joins(left_x[1], left_x[2], low)
        low_own = joins(left_x[2], box_x[head_box[0]], low)
        if not whole:
            return low_pair, low_own
        short = jnp.sum(jnp.where(lane == 7, left_row, 0)) < 3
        third = jnp.where(short, jnp.sum(jnp.where(lane == 3, beside[2], 0)), left_x[0])
        return low_pair, low_own, short, joins(third, left_x[1], low)

    def far_box(slot, start, f, flags):
        low_pair, _, short, low_rim = flags
        at, rim = 32 * f, 32 * fields + 8 * (f // 2)
        left_rim = jnp.where(short, from_second[rim - 32 * fields : rim - 32 * fields + 8, :], from_left[rim : rim + 8, :])
        if f % 2 == 0:
            left_rim = pltpu.roll(left_rim, 4, 0)
        across(slot, start, left_rim, from_left[at : at + 16, :], from_left[at + 16 : at + 24, :], pair(f, low_rim, low_pair))

    def left_part(whole):
        arrive((0, 2) if whole else (0,))
        flags = left_joins(whole)
        low_pair, low_own = flags[:2]

        def x_part(f):
            slot, at = f % 2, 32 * f
            head = held[head_box[0], f, 0:8, :]
            across(slot, 0, from_left[at + 8 : at + 16, :], from_left[at + 16 : at + 32, :], head, pair(f, low_pair, low_own))
            edge = jnp.where(low_own == 1, from_left[at + 24 : at + 32, :], zero)
            across(slot, 32, edge, held[head_box[0], f], held[head_box[0], f, 8:16, :], mats[f, low_own, 0:16, :])
            if whole:
                far_box(slot, 48, f, flags)

        in_turn(x_part, [(1, 0, 32), (2, 0, 16)] + ([(0, 0, 32)] if whole else []))

    def right_part(extra):
        arrive((1, 2) if extra else (1,))
        flags = left_joins(True) if extra else None
        right_row = beside[1]
        high = me < total - 1
        right_x = [jnp.sum(jnp.where(lane == 4 + k, right_row, 0)) for k in range(3)]
        high_own = joins(box_x[tail_box[2]], right_x[0], high)
        high_pair = joins(right_x[0], right_x[1], high)
        high_rim = joins(right_x[1], right_x[2], high)

        def x_part(f):
            slot, at, rim = f % 2, 32 * f, 32 * fields + 8 * (f // 2)
            right_rim = from_right[rim : rim + 8, :]
            if f % 2:
                right_rim = pltpu.roll(right_rim, 4, 0)
            tail = held[tail_box[2], f, 8:16, :]
            across(slot, 0, tail, from_right[at : at + 16, :], from_right[at + 16 : at + 24, :], pair(f, high_own, high_pair))
            across(slot, 32, from_right[at + 8 : at + 16, :], from_right[at + 16 : at + 32, :], right_rim, pair(f, high_pair, high_rim))
            edge = jnp.where(high_own == 1, from_right[at : at + 8, :], zero)
            across(slot, 64, held[tail_box[2], f, 0:8, :], held[tail_box[2], f], edge, mats[f, high_own, 16:32, :])
            if extra:
                far_box(slot, 80, f, flags)

        in_turn(x_part, [(10, 0, 32), (11, 0, 32), (12, 16, 16)] + ([(0, 0, 32)] if extra else []))

    even, turn = sub % 2 == 0, (sub == 1) & (me > 1)

    @pl.when(even)
    def _():
        right_part(False)
        left_part(True)

    @pl.when(turn)
    def _():
        left_part(False)
        right_part(True)

    @pl.when(jnp.logical_not(even | turn))
    def _():
        left_part(True)
        right_part(False)

    keep.wait()
    for o, copy in enumerate(curve_copies):
        pl.when(comes[o])(copy.wait_recv)
    for copy in sub_copies:
        copy.wait_send()
    for o, copy in enumerate(curve_copies):
        pl.when(goes[o])(copy.wait_send)
    for k, (step, sends, gets) in enumerate(chain):
        @pl.when(sends)
        def _(k=k):
            side_copies[k].wait_send()
            box_copies[k].wait_send()


def settle(n_curve, n_sub, all_rows, cand, out, sems):
    boxes = out.shape[0]
    n_half = n_curve // 2
    curve, sub = lax.axis_index("curve"), lax.axis_index("sub")
    shape = all_rows.shape
    order = lax.broadcasted_iota(jnp.int32, shape, 0)
    lanes = lax.broadcasted_iota(jnp.int32, shape, 1)
    spot = (curve % n_half) * n_sub + sub
    rows = all_rows[...]
    below = jnp.where((lanes == 0) & (order < spot), rows, 0)
    above = jnp.where((lanes == 0) & (order >= spot), rows, 0)
    offset = jnp.sum(jnp.where(curve < n_half, below, -above))
    change = jnp.sum(jnp.where((lanes == 0) & (order == spot), rows, 0))
    live = jnp.sum(jnp.where((lanes == 7) & (order == spot), rows, 0))
    copies = []
    for j in range(boxes):
        rank = offset + j
        pick = jnp.where(rank < live - 1, 2 + rank, jnp.where(rank == live - 1, 12, 10 + rank - live))
        pick = jnp.clip(jnp.where(j < live + change, pick, 13), 0, 13)
        copy = pltpu.make_async_copy(cand.at[pick], out.at[j], sems.at[j])
        copy.start()
        copies.append(copy)
    for copy in copies:
        copy.wait()


def local(n_curve, n_sub, coarse, tags, box_x, counts, courant):
    boxes, fields, half, plane = coarse.shape
    fine = 2 * half
    joined, alone = x_tables(half)
    tables = jnp.asarray(plane_tables(half), jnp.bfloat16)
    vmem = pl.BlockSpec(memory_space=pltpu.VMEM)
    anywhere = pl.BlockSpec(memory_space=pl.ANY)
    stay = pl.BlockSpec(memory_space=pltpu.HBM)
    packed = 36 * fields
    dma = pltpu.SemaphoreType.DMA
    n_half = n_curve // 2
    edge = pltpu.VMEM((packed, plane), jnp.float32)
    rim = pltpu.VMEM((4 * fields, plane), jnp.float32)
    inputs = (tags, box_x, courant, coarse, jnp.asarray(joined), jnp.asarray(alone), tables)
    all_rows, cand = pl.pallas_call(
        functools.partial(exchange, n_curve, n_sub),
        out_shape=(
            jax.ShapeDtypeStruct((n_half, n_sub, 1, 128), jnp.int32),
            jax.ShapeDtypeStruct((boxes + 6, fields, fine, 4 * plane), jnp.float32),
        ),
        in_specs=[stay] * 7 + [pl.BlockSpec(memory_space=pltpu.SMEM)],
        out_specs=(vmem, vmem),
        scratch_shapes=[
            pltpu.SMEM((boxes,), jnp.int32),
            pltpu.SMEM((boxes,), jnp.int32),
            pltpu.SMEM((fields,), jnp.float32),
            pltpu.VMEM((48, 128), jnp.float32),
            pltpu.VMEM((40, 128), jnp.float32),
            pltpu.VMEM(tables.shape, jnp.bfloat16),
            pltpu.VMEM((fields, 2, fine, 128), jnp.bfloat16),
            pltpu.VMEM((2, 4, (boxes + 1) * fine, plane), jnp.bfloat16),
            pltpu.VMEM(coarse.shape, jnp.float32),
            edge, edge, rim,
            edge, edge, rim,
            pltpu.VMEM((n_half, n_sub, 1, 128), jnp.int32),
            pltpu.VMEM((3, 1, 128), jnp.int32),
            pltpu.VMEM((48, 128), jnp.float32),
            dma((7,)),
            dma((1,)),
            dma((3,)),
            dma((3,)),
            dma((3,)),
            dma((3,)),
            dma((n_sub - 1,)),
            dma((n_sub - 1,)),
            dma((n_half - 1,)),
            dma((n_half - 1,)),
        ],
        compiler_params=pltpu.CompilerParams(collective_id=0, has_side_effects=True, vmem_limit_bytes=24 * 2**20),
        name="exchange",
    )(*[pltpu.with_memory_space_constraint(a, pltpu.HBM) for a in inputs], counts)
    return pl.pallas_call(
        functools.partial(settle, n_curve, n_sub),
        out_shape=jax.ShapeDtypeStruct((boxes, fields, fine, 4 * plane), jnp.float32),
        in_specs=[vmem, vmem],
        out_specs=anywhere,
        scratch_shapes=[dma((boxes,))],
        compiler_params=pltpu.CompilerParams(vmem_limit_bytes=16 * 2**20),
        name="settle",
    )(all_rows.reshape(n_half * n_sub, 128), cand)


def solution(mesh):
    both = ("curve", "sub")
    in_specs = (P(both, None, None, None), P(both), P(both), P(both), P())
    return jax.shard_map(
        functools.partial(local, mesh.shape["curve"], mesh.shape["sub"]),
        mesh=mesh,
        in_specs=in_specs,
        out_specs=P(both, None, None, None),
        check_vma=False,
    )
```
